128 devices in a mesh: pos: 16 (over x, y), obj: 8 (over z, core).
Axes of the slice: x: 4, y: 4, z: 4, core: 2. Of those that a mesh axis runs over, the one named last changes fastest.
Arguments:
- object_field: float32 [2, 4096, 6144], P(None, 'obj', 'pos'), may hold values from -5 to 5
- probe: float32 [2, 256, 256], replicated, may hold values from -5 to 5
- amplitude: bfloat16 [2048, 256, 256], P(('pos', 'obj')), may hold values from 0.19921875 to 3
- row_offset: int32 [2048], P(('pos', 'obj')), may hold values from 0 to 256
- col_offset: int32 [2048], P(('pos', 'obj')), may hold values from 0 to 128
- owner: int32 [2048], P(('pos', 'obj')), may hold values from 0 to 15, as said below
Outputs:
- new_object: float32 [2, 4096, 6144], P(None, 'obj', 'pos')
- new_probe: float32 [2, 256, 256], replicated
The draws below stay inside these ranges and needn't reach their ends.
Inputs may be any that keep to these rules, and one draw needn't show every extreme that they name: Among the 16 positions of one device no owner is named more than 2 times; in each row band one owner is named exactly 2 times by every device.
All inputs are finite; a program needn't handle non-finite values.
Results may differ from the reference program's by a relative error of at most 0.005.
The reference program's roundings to bfloat16 on the way count: a program that leaves them out, or rounds other values in their place, can miss the bound.
Values may be sent and summed in bfloat16 or wider, within the bound.
A program may use at most 128 MiB of HBM per device.

```python
import math
import jax
import jax.numpy as jnp
from jax import lax

PATCH = 256
TILE_ROWS = 512
TILE_COLS = 384
POS_DEV = 16
CAPACITY = 2
NPOS = 2048
OBJ_ROWS = 4096
OBJ_COLS = 6144
N_POS = 16
N_OBJ = 8


def draw_owner(key, part):
    count = N_POS * N_OBJ
    hottest = jax.random.randint(jax.random.fold_in(key, 1), (N_OBJ,), 0, N_POS)
    block_keys = jax.random.split(jax.random.fold_in(key, 2), count)
    band = jnp.arange(count) % N_OBJ

    def one_block(block_key, hot_owner):
        first, second = jax.random.split(block_key)
        spare = jax.random.permutation(first, (N_POS - 1) * CAPACITY)[:POS_DEV - CAPACITY]
        others = (hot_owner + 1 + spare // CAPACITY) % N_POS
        listed = jnp.concatenate([jnp.full((CAPACITY,), hot_owner, jnp.int32), others.astype(jnp.int32)])
        order = jax.random.permutation(second, POS_DEV)
        return listed[order]
    return jax.vmap(one_block)(block_keys, hottest[band]).reshape(-1).astype(jnp.int32)


def plant(entries, stream_key, smallest, high):
    shape = entries.shape
    spot = [jax.random.randint(jax.random.fold_in(stream_key, axis), (), 0, shape[axis]) for axis in range(len(shape))]
    entries = entries.at[tuple(spot)].set(smallest)
    longest = shape.index(max(shape))
    spot[longest] = (spot[longest] + 1) % shape[longest]
    return entries.at[tuple(spot)].set(high)


def level_of(stream_key, dims, pieces, low, top_value):
    gain = 1.0
    for dim, shards_of in pieces:
        steps = jax.random.uniform(jax.random.fold_in(jax.random.fold_in(stream_key, 6), dim), (shards_of,), jnp.float32, low / len(pieces), top_value / len(pieces))
        gain = gain * jnp.repeat(jnp.exp(steps), dims[dim] // shards_of).reshape((-1,) + (1,) * (len(dims) - 1 - dim))
    return gain


def noise(key, shape, spread, limit, pieces=(), held_as=jnp.bfloat16):
    values = spread * jax.random.normal(key, shape, jnp.float32)
    if pieces:
        values = values * level_of(key, shape, pieces, -0.22, 0.18)
    return jnp.clip(values, -limit, limit).astype(held_as)


def setup_inputs(seed: int = 0) -> dict:
    streams_of = jax.random.split(jax.random.key(seed), 7)
    return {
        "object_field": noise(streams_of[0], (2, OBJ_ROWS, OBJ_COLS), 0.7, 5.0, ((1, 8), (2, 16)), jnp.float32),
        "probe": noise(streams_of[1], (2, PATCH, PATCH), 0.7, 5.0, (), jnp.float32),
        "amplitude": jnp.clip(jnp.exp(math.log(3.0) - 2.7119641 * jax.random.uniform(streams_of[2], (NPOS, PATCH, PATCH), jnp.float32) ** level_of(streams_of[2], (NPOS, PATCH, PATCH), ((0, 128),), -0.2, 0.2)), 0.19921875, 3.0).astype(jnp.bfloat16),
        "row_offset": plant(jax.random.randint(streams_of[3], (NPOS,), 0, TILE_ROWS - PATCH + 1), jax.random.fold_in(streams_of[3], 1), 0, TILE_ROWS - PATCH).astype(jnp.int32),
        "col_offset": plant(jax.random.randint(streams_of[4], (NPOS,), 0, TILE_COLS - PATCH + 1), jax.random.fold_in(streams_of[4], 1), 0, TILE_COLS - PATCH).astype(jnp.int32),
        "owner": draw_owner(jax.random.fold_in(streams_of[6], 71), 0),
    }


def dft_tables(size):
    index = jnp.arange(size, dtype=jnp.int32)
    product = index[:, None] * index[None, :] % size
    angle = product.astype(jnp.float32) * (2.0 * math.pi / size)
    scale = 1.0 / math.sqrt(size)
    real_part = (jnp.cos(angle) * scale).astype(jnp.bfloat16)
    imag_part = (-jnp.sin(angle) * scale).astype(jnp.bfloat16)
    return (real_part, imag_part)

def left_apply(mat_re, mat_im, val_re, val_im):

    def product(matrix, values):
        return jnp.einsum('jk,bkl->bjl', matrix.astype(jnp.float32), values.astype(jnp.float32), precision=lax.Precision.HIGHEST)
    return (product(mat_re, val_re) - product(mat_im, val_im), product(mat_re, val_im) + product(mat_im, val_re))

def right_apply(val_re, val_im, mat_re, mat_im):

    def product(values, matrix):
        return jnp.einsum('bjk,kl->bjl', values.astype(jnp.float32), matrix.astype(jnp.float32), precision=lax.Precision.HIGHEST)
    return (product(val_re, mat_re) - product(val_im, mat_im), product(val_re, mat_im) + product(val_im, mat_re))

def position_terms(patches, amps, probe, four_re, four_im, conj_im):
    patch_re = patches[:, 0].astype(jnp.float32)
    patch_im = patches[:, 1].astype(jnp.float32)
    probe_re = probe[0]
    probe_im = probe[1]
    psi_re = (probe_re * patch_re - probe_im * patch_im).astype(jnp.bfloat16)
    psi_im = (probe_re * patch_im + probe_im * patch_re).astype(jnp.bfloat16)
    left_re, left_im = left_apply(four_re, four_im, psi_re, psi_im)
    wave_re, wave_im = right_apply(left_re.astype(jnp.bfloat16), left_im.astype(jnp.bfloat16), four_re, four_im)
    magnitude = jnp.sqrt(wave_re * wave_re + wave_im * wave_im)
    factor = 1.0 - amps.astype(jnp.float32) / jnp.maximum(magnitude, 0.5)
    diff_re = (wave_re * factor).astype(jnp.bfloat16)
    diff_im = (wave_im * factor).astype(jnp.bfloat16)
    back_re, back_im = left_apply(four_re, conj_im, diff_re, diff_im)
    chi_re, chi_im = right_apply(back_re.astype(jnp.bfloat16), back_im.astype(jnp.bfloat16), four_re, conj_im)
    grad_re = (probe_re * chi_re + probe_im * chi_im).astype(jnp.bfloat16)
    grad_im = (probe_re * chi_im - probe_im * chi_re).astype(jnp.bfloat16)
    term_re = lax.optimization_barrier(jnp.sum(patch_re * chi_re + patch_im * chi_im, axis=0))
    term_im = lax.optimization_barrier(jnp.sum(patch_re * chi_im - patch_im * chi_re, axis=0))
    return (jnp.stack([grad_re, grad_im], axis=1), jnp.stack([term_re, term_im]))

def reference(object_field, probe, amplitude, row_offset, col_offset, owner):
    npos = amplitude.shape[0]
    size = amplitude.shape[1]
    index = jnp.arange(npos, dtype=jnp.int32)
    band = index // POS_DEV % N_OBJ
    rows = (band * TILE_ROWS + row_offset).astype(jnp.int32)
    cols = (owner * TILE_COLS + col_offset).astype(jnp.int32)
    four_re, four_im = dft_tables(size)
    conj_im = -four_im
    zero = jnp.zeros((), jnp.int32)

    def step(carry, block):
        grad_obj, probe_acc = carry
        start = (block * POS_DEV).astype(jnp.int32)
        row_here = lax.dynamic_slice_in_dim(rows, start, POS_DEV, 0)
        col_here = lax.dynamic_slice_in_dim(cols, start, POS_DEV, 0)
        patches = jax.vmap(lambda row, col: lax.dynamic_slice(object_field, (zero, row, col), (2, size, size)))(row_here, col_here).astype(jnp.bfloat16)
        amps = lax.dynamic_slice_in_dim(amplitude, start, POS_DEV, 0)
        grads, term = position_terms(patches, amps, probe, four_re, four_im, conj_im)

        def add_one(item, acc):
            corner = (zero, row_here[item], col_here[item])
            window = lax.dynamic_slice(acc, corner, (2, size, size))
            return lax.dynamic_update_slice(acc, window + grads[item].astype(jnp.float32), corner)
        grad_obj = lax.fori_loop(0, POS_DEV, add_one, grad_obj)
        return ((grad_obj, probe_acc + term), None)
    blocks = jnp.arange(npos // POS_DEV, dtype=jnp.int32)
    start_carry = (jnp.zeros(object_field.shape, jnp.float32), jnp.zeros(probe.shape, jnp.float32))
    (object_grad, probe_grad), _ = lax.scan(step, start_carry, blocks)
    smooth = 4.0 * object_field - jnp.roll(object_field, 1, 1) - jnp.roll(object_field, -1, 1)
    smooth = smooth - jnp.roll(object_field, 1, 2) - jnp.roll(object_field, -1, 2)
    new_object = object_field - 0.25 * (object_grad + 0.5 * smooth)
    new_probe = probe - probe_grad * (1.0 / math.sqrt(npos))
    return (new_object, new_probe)
```

```python
import functools
import math

import jax
import jax.numpy as jnp
import numpy as np
from jax import lax
from jax.experimental import pallas as pl
from jax.experimental.pallas import tpu as pltpu
from jax.sharding import PartitionSpec as P

SIZE = 256
CAPACITY = 2
LANES = 128
F32 = jnp.float32
BF16 = jnp.bfloat16


def dft_blocks():
    index = np.arange(SIZE, dtype=np.int64)
    product = (index[:, None] * index[None, :]) % SIZE
    angle = product.astype(np.float32) * np.float32(2.0 * math.pi / SIZE)
    scale = 1.0 / math.sqrt(SIZE)
    real = (np.cos(angle.astype(np.float64)) * scale).astype(np.float32)
    imag = (-np.sin(angle.astype(np.float64)) * scale).astype(np.float32)
    real = jnp.asarray(real).astype(BF16)
    imag = jnp.asarray(imag).astype(BF16)
    top = jnp.concatenate([real, -imag], axis=1)
    bottom = jnp.concatenate([imag, real], axis=1)
    left = jnp.concatenate([top, bottom], axis=0)
    top = jnp.concatenate([real, imag], axis=1)
    bottom = jnp.concatenate([-imag, real], axis=1)
    return left, jnp.concatenate([top, bottom], axis=0)


def pack_kernel(n_pos, owner, rows, cols, amps, slots, meta, source, count, sems):
    total = n_pos * CAPACITY
    n_dev = owner.shape[0]

    @pl.loop(0, n_pos)
    def _(i):
        count[i] = 0

    @pl.loop(0, total)
    def _(i):
        source[i] = 0
        meta[i, 0] = 2 * SIZE
        meta[i, 1] = 0

    @pl.loop(0, n_dev)
    def _(i):
        o = owner[i]
        k = count[o]
        count[o] = k + 1
        slot = k * n_pos + o
        source[slot] = i
        meta[slot, 0] = rows[i]
        meta[slot, 1] = cols[i]

    @pl.loop(0, total)
    def _(i):
        pltpu.make_async_copy(amps.at[source[i]], slots.at[i], sems.at[i]).start()

    @pl.loop(0, total)
    def _(i):
        pltpu.make_async_copy(amps.at[source[i]], slots.at[i], sems.at[i]).wait()


def pack(owner, rows, cols, amps, n_pos):
    total = n_pos * CAPACITY
    smem = pl.BlockSpec(memory_space=pltpu.SMEM)
    hbm = pl.BlockSpec(memory_space=pl.ANY)
    return pl.pallas_call(
        functools.partial(pack_kernel, n_pos),
        out_shape=(
            jax.ShapeDtypeStruct((total, SIZE, SIZE), BF16),
            jax.ShapeDtypeStruct((total, 2), jnp.int32),
        ),
        in_specs=[smem, smem, smem, hbm],
        out_specs=(hbm, smem),
        scratch_shapes=[
            pltpu.SMEM((total,), jnp.int32),
            pltpu.SMEM((n_pos,), jnp.int32),
            pltpu.SemaphoreType.DMA((total,)),
        ],
        name="pack",
    )(owner, rows, cols, amps)


STRIP = 32


def extract(meta_row, meta_col, tile, probe, window, psi, j):
    lane = lax.broadcasted_iota(jnp.int32, (STRIP, LANES), 1)
    first = lane < LANES - meta_col
    shift = lax.rem(LANES - meta_col, LANES)
    for s in range(0, SIZE, STRIP):
        parts = []
        for p in range(2):
            t = [
                pltpu.roll(tile[p, k, pl.ds(meta_row + s, STRIP), :], shift, 1)
                for k in range(3)
            ]
            parts.append([jnp.where(first, t[k], t[k + 1]) for k in range(2)])
        for k in range(2):
            cols = slice(k * LANES, (k + 1) * LANES)
            x_re, x_im = parts[0][k], parts[1][k]
            window[j, 0, s : s + STRIP, cols] = x_re
            window[j, 1, s : s + STRIP, cols] = x_im
            p_re = probe[0, s : s + STRIP, cols]
            p_im = probe[1, s : s + STRIP, cols]
            out = slice(j * SIZE + k * LANES, j * SIZE + (k + 1) * LANES)
            psi[s : s + STRIP, out] = (p_re * x_re - p_im * x_im).astype(BF16)
            psi[SIZE + s : SIZE + s + STRIP, out] = (p_re * x_im + p_im * x_re).astype(BF16)


def turn(value, out):
    for j in range(2):
        for part in range(2):
            out[j * SIZE : (j + 1) * SIZE, part * SIZE : (part + 1) * SIZE] = value[
                part * SIZE : (part + 1) * SIZE, j * SIZE : (j + 1) * SIZE
            ].astype(BF16)


def modulus(wave, amp, diff, j):
    for s in range(0, SIZE, STRIP):
        rows = slice(j * SIZE + s, j * SIZE + s + STRIP)
        w_re = wave[rows, 0:SIZE]
        w_im = wave[rows, SIZE : 2 * SIZE]
        a = amp[j, s : s + STRIP, :].astype(F32)
        power = w_re * w_re + w_im * w_im
        factor = 1.0 - a * lax.rsqrt(jnp.maximum(power, 0.25))
        cols = slice(j * SIZE, (j + 1) * SIZE)
        diff[s : s + STRIP, cols] = (w_re * factor).astype(BF16)
        diff[SIZE + s : SIZE + s + STRIP, cols] = (w_im * factor).astype(BF16)


def gather_back(meta_row, meta_col, chi, probe, window, acc, term, j):
    lane = lax.broadcasted_iota(jnp.int32, (STRIP, LANES), 1)
    later = lane >= meta_col
    shift = lax.rem(meta_col, LANES)
    row = jnp.bitwise_and(meta_row, 2 * SIZE - 1)
    zero = jnp.zeros((STRIP, LANES), F32)
    for s in range(0, SIZE, STRIP):
        rows = slice(j * SIZE + s, j * SIZE + s + STRIP)
        turned = [[], []]
        for k in range(2):
            cols = slice(k * LANES, (k + 1) * LANES)
            c_re = chi[rows, k * LANES : (k + 1) * LANES]
            c_im = chi[rows, SIZE + k * LANES : SIZE + (k + 1) * LANES]
            x_re = window[j, 0, s : s + STRIP, cols]
            x_im = window[j, 1, s : s + STRIP, cols]
            term[0, s : s + STRIP, cols] += x_re * c_re + x_im * c_im
            term[1, s : s + STRIP, cols] += x_re * c_im - x_im * c_re
            p_re = probe[0, s : s + STRIP, cols]
            p_im = probe[1, s : s + STRIP, cols]
            g_re = (p_re * c_re + p_im * c_im).astype(BF16).astype(F32)
            g_im = (p_re * c_im - p_im * c_re).astype(BF16).astype(F32)
            turned[0].append(pltpu.roll(g_re, shift, 1))
            turned[1].append(pltpu.roll(g_im, shift, 1))
        for p in range(2):
            low, high = turned[p]
            here = pl.ds(row + s, STRIP)
            acc[p, 0, here, :] += jnp.where(later, low, zero)
            acc[p, 1, here, :] += jnp.where(later, high, low)
            acc[p, 2, here, :] += jnp.where(later, zero, high)


def compute_kernel(
    first_call, last_call, n_steps,
    meta, obj, probe, left, right, amp, acc_in, term_in, base,
    out, term, tile, window, psi, half, wave, diff, chi, acc,
):
    step = pl.program_id(0)

    @pl.when(step == 0)
    def _():
        for p in range(2):
            for k in range(3):
                cols = slice(k * LANES, (k + 1) * LANES)
                tile[p, k, 0 : 2 * SIZE, :] = obj[p, :, cols].astype(BF16).astype(F32)
                tile[p, k, 2 * SIZE : 3 * SIZE, :] = jnp.zeros((SIZE, LANES), F32)
        if first_call:
            acc[...] = jnp.zeros_like(acc)
            term[...] = jnp.zeros_like(term)
        else:
            acc[...] = acc_in[...]
            term[...] = term_in[...]

    row = [meta[2 * step + j, 0] for j in range(2)]
    col = [meta[2 * step + j, 1] for j in range(2)]

    @pl.when(jnp.minimum(row[0], row[1]) < 2 * SIZE)
    def _():
        for j in range(2):
            extract(row[j], col[j], tile, probe, window, psi, j)
        turn(jnp.dot(left[...], psi[...], preferred_element_type=F32), half)
        wave[...] = jnp.dot(half[...], right[...], preferred_element_type=F32)
        for j in range(2):
            modulus(wave, amp, diff, j)
        turn(jnp.dot(right[...], diff[...], preferred_element_type=F32), half)
        chi[...] = jnp.dot(half[...], left[...], preferred_element_type=F32)
        for j in range(2):
            gather_back(row[j], col[j], chi, probe, window, acc, term, j)

    @pl.when(step == n_steps - 1)
    def _():
        if last_call:
            for p in range(2):
                for k in range(3):
                    cols = slice(k * LANES, (k + 1) * LANES)
                    out[p, :, cols] = base[p, :, cols] - 0.25 * acc[p, k]
        else:
            out[...] = acc[...]


def compute(first_call, last_call, meta, obj, probe, left, right, amp, acc_in, term_in, base):
    count = amp.shape[0]
    n_steps = count // 2
    whole = lambda *shape: pl.BlockSpec(shape, lambda i: (0,) * len(shape))
    dummy = pl.BlockSpec(memory_space=pl.ANY)
    panels = (2, 3, 2 * SIZE, LANES)
    acc_spec = dummy if first_call else whole(*panels)
    term_spec = dummy if first_call else whole(2, SIZE, SIZE)
    base_spec = whole(*obj.shape) if last_call else dummy
    out_shape = obj.shape if last_call else panels
    flops = count * 16 * 2 * SIZE**3
    return pl.pallas_call(
        functools.partial(compute_kernel, first_call, last_call, n_steps),
        grid=(n_steps,),
        out_shape=(
            jax.ShapeDtypeStruct(out_shape, F32),
            jax.ShapeDtypeStruct((2, SIZE, SIZE), F32),
        ),
        in_specs=[
            pl.BlockSpec(memory_space=pltpu.SMEM),
            whole(*obj.shape),
            whole(2, SIZE, SIZE),
            whole(2 * SIZE, 2 * SIZE),
            whole(2 * SIZE, 2 * SIZE),
            pl.BlockSpec((2, SIZE, SIZE), lambda i: (i, 0, 0)),
            acc_spec,
            term_spec,
            base_spec,
        ],
        out_specs=(whole(*out_shape), whole(2, SIZE, SIZE)),
        scratch_shapes=[
            pltpu.VMEM((2, 3, 3 * SIZE, LANES), F32),
            pltpu.VMEM((2, 2, SIZE, SIZE), F32),
            pltpu.VMEM((2 * SIZE, 2 * SIZE), BF16),
            pltpu.VMEM((2 * SIZE, 2 * SIZE), BF16),
            pltpu.VMEM((2 * SIZE, 2 * SIZE), F32),
            pltpu.VMEM((2 * SIZE, 2 * SIZE), BF16),
            pltpu.VMEM((2 * SIZE, 2 * SIZE), F32),
            pltpu.VMEM(panels, F32),
        ],
        compiler_params=pltpu.CompilerParams(
            dimension_semantics=("arbitrary",), vmem_limit_bytes=56 << 20
        ),
        cost_estimate=pl.CostEstimate(flops=flops, bytes_accessed=16 << 20, transcendentals=0),
        name="positions",
    )(meta, obj, probe, left, right, amp, acc_in, term_in, base)


def exchanged(block, axis, dim):
    count = lax.axis_size(axis)
    forward = [(i, (i + 1) % count) for i in range(count)]
    backward = [(target, source) for source, target in forward]
    size = block.shape[dim]
    low = lax.ppermute(lax.slice_in_dim(block, size - 1, size, axis=dim), axis, forward)
    high = lax.ppermute(lax.slice_in_dim(block, 0, 1, axis=dim), axis, backward)
    return jnp.concatenate([low, block, high], axis=dim)


def shards(object_field, probe, amplitude, row_offset, col_offset, owner):
    n_pos = lax.axis_size("pos")
    n_obj = lax.axis_size("obj")
    pos_dev = amplitude.shape[0]
    left, right = dft_blocks()
    slots, meta = pack(owner, row_offset, col_offset, amplitude, n_pos)
    arrived = [
        lax.all_to_all(slots[k * n_pos : (k + 1) * n_pos], "pos", 0, 0, tiled=True)
        for k in range(CAPACITY)
    ]
    corners = lax.all_to_all(meta.reshape(CAPACITY, n_pos, 2), "pos", 1, 1, tiled=True)
    tall = exchanged(object_field, "obj", 1)
    wide = exchanged(object_field, "pos", 2)
    smooth = 4.0 * object_field - tall[:, :-2] - tall[:, 2:] - wide[:, :, :-2] - wide[:, :, 2:]
    base = object_field - 0.125 * smooth
    none = jnp.zeros((8, 128), F32)
    acc, term = compute(
        True, False, corners[0], object_field, probe, left, right, arrived[0], none, none, none
    )
    new_object, term = compute(
        False, True, corners[1], object_field, probe, left, right, arrived[1], acc, term, base
    )
    probe_grad = lax.psum(term, ("pos", "obj"))
    n_total = pos_dev * n_pos * n_obj
    return new_object, probe - probe_grad * (1.0 / math.sqrt(n_total))


def solution(mesh):
    placed = (
        P(None, "obj", "pos"),
        P(),
        P(("pos", "obj"), None, None),
        P(("pos", "obj")),
        P(("pos", "obj")),
        P(("pos", "obj")),
    )
    return jax.shard_map(
        shards, mesh=mesh, in_specs=placed, out_specs=(P(None, "obj", "pos"), P()), check_vma=False
    )
```

```python
import functools
import math

import jax
import jax.numpy as jnp
import numpy as np
from jax import lax
from jax.experimental import pallas as pl
from jax.experimental.pallas import tpu as pltpu
from jax.sharding import PartitionSpec as P

SIZE = 256
CAPACITY = 2
LANES = 128
F32 = jnp.float32
BF16 = jnp.bfloat16


def dft_blocks():
    index = np.arange(SIZE, dtype=np.int64)
    product = (index[:, None] * index[None, :]) % SIZE
    angle = product.astype(np.float32) * np.float32(2.0 * math.pi / SIZE)
    scale = 1.0 / math.sqrt(SIZE)
    real = (np.cos(angle.astype(np.float64)) * scale).astype(np.float32)
    imag = (-np.sin(angle.astype(np.float64)) * scale).astype(np.float32)
    real = jnp.asarray(real).astype(BF16)
    imag = jnp.asarray(imag).astype(BF16)
    top = jnp.concatenate([real, -imag], axis=1)
    bottom = jnp.concatenate([imag, real], axis=1)
    left = jnp.concatenate([top, bottom], axis=0)
    top = jnp.concatenate([real, imag], axis=1)
    bottom = jnp.concatenate([-imag, real], axis=1)
    return left, jnp.concatenate([top, bottom], axis=0)


def pack_kernel(n_pos, owner, rows, cols, amps, slots, meta, source, count):
    total = n_pos * CAPACITY
    n_dev = owner.shape[0]

    @pl.loop(0, n_pos)
    def _(i):
        count[i] = 0

    @pl.loop(0, total)
    def _(i):
        source[i] = 0
        meta[i, 0] = 2 * SIZE
        meta[i, 1] = 0

    @pl.loop(0, n_dev)
    def _(i):
        o = owner[i]
        k = count[o]
        count[o] = k + 1
        slot = k * n_pos + o
        source[slot] = i
        meta[slot, 0] = rows[i]
        meta[slot, 1] = cols[i]

    @pl.loop(0, total)
    def _(i):
        slots[i] = amps[source[i]]


def pack(owner, rows, cols, amps, n_pos):
    total = n_pos * CAPACITY
    smem = pl.BlockSpec(memory_space=pltpu.SMEM)
    vmem = pl.BlockSpec(memory_space=pltpu.VMEM)
    return pl.pallas_call(
        functools.partial(pack_kernel, n_pos),
        out_shape=(
            jax.ShapeDtypeStruct((total, SIZE, SIZE), BF16),
            jax.ShapeDtypeStruct((total, 2), jnp.int32),
        ),
        in_specs=[smem, smem, smem, vmem],
        out_specs=(vmem, smem),
        scratch_shapes=[
            pltpu.SMEM((total,), jnp.int32),
            pltpu.SMEM((n_pos,), jnp.int32),
        ],
        compiler_params=pltpu.CompilerParams(vmem_limit_bytes=24 << 20),
        name="pack",
    )(owner, rows, cols, amps)


STRIP = 32


def extract(meta_row, meta_col, tile, probe, window, psi, j):
    lane = lax.broadcasted_iota(jnp.int32, (STRIP, LANES), 1)
    first = lane < LANES - meta_col
    shift = lax.rem(LANES - meta_col, LANES)
    for s in range(0, SIZE, STRIP):
        parts = []
        for p in range(2):
            t = [
                pltpu.roll(tile[p, k, pl.ds(meta_row + s, STRIP), :], shift, 1)
                for k in range(3)
            ]
            parts.append([jnp.where(first, t[k], t[k + 1]) for k in range(2)])
        for k in range(2):
            cols = slice(k * LANES, (k + 1) * LANES)
            x_re, x_im = parts[0][k], parts[1][k]
            window[j, 0, s : s + STRIP, cols] = x_re
            window[j, 1, s : s + STRIP, cols] = x_im
            p_re = probe[0, s : s + STRIP, cols]
            p_im = probe[1, s : s + STRIP, cols]
            out = slice(j * SIZE + k * LANES, j * SIZE + (k + 1) * LANES)
            psi[s : s + STRIP, out] = (p_re * x_re - p_im * x_im).astype(BF16)
            psi[SIZE + s : SIZE + s + STRIP, out] = (p_re * x_im + p_im * x_re).astype(BF16)


def turn(value, out):
    for j in range(2):
        for part in range(2):
            out[j * SIZE : (j + 1) * SIZE, part * SIZE : (part + 1) * SIZE] = value[
                part * SIZE : (part + 1) * SIZE, j * SIZE : (j + 1) * SIZE
            ].astype(BF16)


def modulus(wave, amp, diff, j):
    for s in range(0, SIZE, STRIP):
        rows = slice(j * SIZE + s, j * SIZE + s + STRIP)
        w_re = wave[rows, 0:SIZE]
        w_im = wave[rows, SIZE : 2 * SIZE]
        a = amp[j, s : s + STRIP, :].astype(F32)
        power = w_re * w_re + w_im * w_im
        factor = 1.0 - a * lax.rsqrt(jnp.maximum(power, 0.25))
        cols = slice(j * SIZE, (j + 1) * SIZE)
        diff[s : s + STRIP, cols] = (w_re * factor).astype(BF16)
        diff[SIZE + s : SIZE + s + STRIP, cols] = (w_im * factor).astype(BF16)


def gather_back(meta_row, meta_col, chi, probe, window, acc, term, j):
    lane = lax.broadcasted_iota(jnp.int32, (STRIP, LANES), 1)
    later = lane >= meta_col
    shift = lax.rem(meta_col, LANES)
    row = jnp.bitwise_and(meta_row, 2 * SIZE - 1)
    zero = jnp.zeros((STRIP, LANES), F32)
    for s in range(0, SIZE, STRIP):
        rows = slice(j * SIZE + s, j * SIZE + s + STRIP)
        turned = [[], []]
        for k in range(2):
            cols = slice(k * LANES, (k + 1) * LANES)
            c_re = chi[rows, k * LANES : (k + 1) * LANES]
            c_im = chi[rows, SIZE + k * LANES : SIZE + (k + 1) * LANES]
            x_re = window[j, 0, s : s + STRIP, cols]
            x_im = window[j, 1, s : s + STRIP, cols]
            term[0, s : s + STRIP, cols] += x_re * c_re + x_im * c_im
            term[1, s : s + STRIP, cols] += x_re * c_im - x_im * c_re
            p_re = probe[0, s : s + STRIP, cols]
            p_im = probe[1, s : s + STRIP, cols]
            g_re = (p_re * c_re + p_im * c_im).astype(BF16).astype(F32)
            g_im = (p_re * c_im - p_im * c_re).astype(BF16).astype(F32)
            turned[0].append(pltpu.roll(g_re, shift, 1))
            turned[1].append(pltpu.roll(g_im, shift, 1))
        for p in range(2):
            low, high = turned[p]
            here = pl.ds(row + s, STRIP)
            acc[p, 0, here, :] += jnp.where(later, low, zero)
            acc[p, 1, here, :] += jnp.where(later, high, low)
            acc[p, 2, here, :] += jnp.where(later, zero, high)


def compute_kernel(
    first_call, last_call, n_steps,
    meta, obj, probe, left, right, amp, acc_in, term_in, base,
    out, term, tile, window, psi, half, wave, diff, chi, acc,
):
    step = pl.program_id(0)

    @pl.when(step == 0)
    def _():
        for p in range(2):
            for k in range(3):
                cols = slice(k * LANES, (k + 1) * LANES)
                tile[p, k, 0 : 2 * SIZE, :] = obj[p, :, cols].astype(BF16).astype(F32)
                tile[p, k, 2 * SIZE : 3 * SIZE, :] = jnp.zeros((SIZE, LANES), F32)
        if first_call:
            acc[...] = jnp.zeros_like(acc)
            term[...] = jnp.zeros_like(term)
        else:
            acc[...] = acc_in[...]
            term[...] = term_in[...]

    row = [meta[2 * step + j, 0] for j in range(2)]
    col = [meta[2 * step + j, 1] for j in range(2)]

    @pl.when(jnp.minimum(row[0], row[1]) < 2 * SIZE)
    def _():
        for j in range(2):
            extract(row[j], col[j], tile, probe, window, psi, j)
        turn(jnp.dot(left[...], psi[...], preferred_element_type=F32), half)
        wave[...] = jnp.dot(half[...], right[...], preferred_element_type=F32)
        for j in range(2):
            modulus(wave, amp, diff, j)
        turn(jnp.dot(right[...], diff[...], preferred_element_type=F32), half)
        chi[...] = jnp.dot(half[...], left[...], preferred_element_type=F32)
        for j in range(2):
            gather_back(row[j], col[j], chi, probe, window, acc, term, j)

    @pl.when(step == n_steps - 1)
    def _():
        if last_call:
            for p in range(2):
                for k in range(3):
                    cols = slice(k * LANES, (k + 1) * LANES)
                    out[p, :, cols] = base[p, :, cols] - 0.25 * acc[p, k]
        else:
            out[...] = acc[...]


def compute(first_call, last_call, meta, obj, probe, left, right, amp, acc_in, term_in, base):
    count = amp.shape[0]
    n_steps = count // 2
    whole = lambda *shape: pl.BlockSpec(shape, lambda i: (0,) * len(shape))
    dummy = pl.BlockSpec(memory_space=pl.ANY)
    panels = (2, 3, 2 * SIZE, LANES)
    acc_spec = dummy if first_call else whole(*panels)
    term_spec = dummy if first_call else whole(2, SIZE, SIZE)
    base_spec = whole(*obj.shape) if last_call else dummy
    out_shape = obj.shape if last_call else panels
    flops = count * 16 * 2 * SIZE**3
    return pl.pallas_call(
        functools.partial(compute_kernel, first_call, last_call, n_steps),
        grid=(n_steps,),
        out_shape=(
            jax.ShapeDtypeStruct(out_shape, F32),
            jax.ShapeDtypeStruct((2, SIZE, SIZE), F32),
        ),
        in_specs=[
            pl.BlockSpec(memory_space=pltpu.SMEM),
            whole(*obj.shape),
            whole(2, SIZE, SIZE),
            whole(2 * SIZE, 2 * SIZE),
            whole(2 * SIZE, 2 * SIZE),
            pl.BlockSpec((2, SIZE, SIZE), lambda i: (i, 0, 0)),
            acc_spec,
            term_spec,
            base_spec,
        ],
        out_specs=(whole(*out_shape), whole(2, SIZE, SIZE)),
        scratch_shapes=[
            pltpu.VMEM((2, 3, 3 * SIZE, LANES), F32),
            pltpu.VMEM((2, 2, SIZE, SIZE), F32),
            pltpu.VMEM((2 * SIZE, 2 * SIZE), BF16),
            pltpu.VMEM((2 * SIZE, 2 * SIZE), BF16),
            pltpu.VMEM((2 * SIZE, 2 * SIZE), F32),
            pltpu.VMEM((2 * SIZE, 2 * SIZE), BF16),
            pltpu.VMEM((2 * SIZE, 2 * SIZE), F32),
            pltpu.VMEM(panels, F32),
        ],
        compiler_params=pltpu.CompilerParams(
            dimension_semantics=("arbitrary",), vmem_limit_bytes=56 << 20
        ),
        cost_estimate=pl.CostEstimate(flops=flops, bytes_accessed=16 << 20, transcendentals=0),
        name="positions",
    )(meta, obj, probe, left, right, amp, acc_in, term_in, base)


MESH = pl.DeviceIdType.MESH


def sum_kernel(n_pos, n_obj, scale, term, probe, out, tiles, got_obj, part, got_pos, done, send, recv):
    me_p = lax.axis_index("pos")
    me_o = lax.axis_index("obj")
    peer_o = [lax.rem(me_o + d, n_obj) for d in range(1, n_obj)]
    peer_p = [lax.rem(me_p + d, n_pos) for d in range(1, n_pos)]

    barrier = pltpu.get_barrier_semaphore()
    for o in peer_o:
        pl.semaphore_signal(barrier, inc=1, device_id=(me_p, o), device_id_type=MESH)
    for p in peer_p:
        pl.semaphore_signal(barrier, inc=1, device_id=(p, me_o), device_id_type=MESH)
    pl.semaphore_wait(barrier, n_obj + n_pos - 2)

    for part_i in range(2):
        for i in range(SIZE // 8):
            for k in range(2):
                tiles[(part_i * (SIZE // 8) + i) * 2 + k] = term[
                    part_i, 8 * i : 8 * i + 8, k * LANES : (k + 1) * LANES
                ]

    def over_obj(base, source_of, target_of):
        return [
            pltpu.make_async_remote_copy(
                src_ref=source_of(d, o), dst_ref=target_of(d, o),
                send_sem=send.at[base + d], recv_sem=recv.at[base + d],
                device_id=(me_p, o), device_id_type=MESH,
            )
            for d, o in enumerate(peer_o)
        ]

    def over_pos(base, source_of, target_of):
        return [
            pltpu.make_async_remote_copy(
                src_ref=source_of(d, p), dst_ref=target_of(d, p),
                send_sem=send.at[base + d], recv_sem=recv.at[base + d],
                device_id=(p, me_o), device_id_type=MESH,
            )
            for d, p in enumerate(peer_p)
        ]

    step = n_obj - 1 + n_pos - 1
    copies = over_obj(0, lambda d, o: tiles.at[pl.ds(o * n_pos, n_pos)], lambda d, o: got_obj.at[d])
    for c in copies:
        c.start()
    for c in copies:
        c.wait_recv()
    total = tiles[pl.ds(me_o * n_pos, n_pos)]
    for d in range(n_obj - 1):
        total += got_obj[d]
    part[...] = total
    second = over_pos(n_obj - 1, lambda d, p: part.at[p], lambda d, p: got_pos.at[d])
    for c in second:
        c.start()
    for c in second:
        c.wait_recv()
    total = part[me_p]
    for d in range(n_pos - 1):
        total += got_pos[d]
    mine = me_o * n_pos + me_p
    done[mine] = total
    third = over_pos(step, lambda d, p: done.at[mine], lambda d, p: done.at[mine])
    for c in third:
        c.start()
    for c in third:
        c.wait_recv()
    block = pl.ds(me_o * n_pos, n_pos)
    fourth = over_obj(step + n_pos - 1, lambda d, o: done.at[block], lambda d, o: done.at[block])
    for c in fourth:
        c.start()
    for c in fourth:
        c.wait_recv()
    for c in copies + second + third + fourth:
        c.wait_send()
    for part_i in range(2):
        for i in range(SIZE // 8):
            for k in range(2):
                rows, cols = slice(8 * i, 8 * i + 8), slice(k * LANES, (k + 1) * LANES)
                out[part_i, rows, cols] = probe[part_i, rows, cols] - scale * done[
                    (part_i * (SIZE // 8) + i) * 2 + k
                ]


def summed(term, probe, n_pos, n_obj, scale):
    count = 2 * (n_pos + n_obj - 2)
    vmem = pl.BlockSpec(memory_space=pltpu.VMEM)
    tiles = n_pos * n_obj
    return pl.pallas_call(
        functools.partial(sum_kernel, n_pos, n_obj, scale),
        out_shape=jax.ShapeDtypeStruct(probe.shape, F32),
        in_specs=[vmem, vmem],
        out_specs=vmem,
        scratch_shapes=[
            pltpu.VMEM((tiles, 8, LANES), F32),
            pltpu.VMEM((n_obj - 1, n_pos, 8, LANES), F32),
            pltpu.VMEM((n_pos, 8, LANES), F32),
            pltpu.VMEM((n_pos - 1, 8, LANES), F32),
            pltpu.VMEM((tiles, 8, LANES), F32),
            pltpu.SemaphoreType.DMA((count,)),
            pltpu.SemaphoreType.DMA((count,)),
        ],
        compiler_params=pltpu.CompilerParams(collective_id=1, has_side_effects=True),
        name="probe_sum",
    )(term, probe)


def exchanged(block, axis, dim):
    count = lax.axis_size(axis)
    forward = [(i, (i + 1) % count) for i in range(count)]
    backward = [(target, source) for source, target in forward]
    size = block.shape[dim]
    low = lax.ppermute(lax.slice_in_dim(block, size - 1, size, axis=dim), axis, forward)
    high = lax.ppermute(lax.slice_in_dim(block, 0, 1, axis=dim), axis, backward)
    return jnp.concatenate([low, block, high], axis=dim)


def shards(object_field, probe, amplitude, row_offset, col_offset, owner):
    n_pos = lax.axis_size("pos")
    n_obj = lax.axis_size("obj")
    pos_dev = amplitude.shape[0]
    left, right = dft_blocks()
    slots, meta = pack(owner, row_offset, col_offset, amplitude, n_pos)
    arrived = [
        lax.all_to_all(slots[k * n_pos : (k + 1) * n_pos], "pos", 0, 0, tiled=True)
        for k in range(CAPACITY)
    ]
    corners = lax.all_to_all(meta.reshape(CAPACITY, n_pos, 2), "pos", 1, 1, tiled=True)
    tall = exchanged(object_field, "obj", 1)
    wide = exchanged(object_field, "pos", 2)
    smooth = 4.0 * object_field - tall[:, :-2] - tall[:, 2:] - wide[:, :, :-2] - wide[:, :, 2:]
    base = object_field - 0.125 * smooth
    none = jnp.zeros((8, 128), F32)
    acc, term = compute(
        True, False, corners[0], object_field, probe, left, right, arrived[0], none, none, none
    )
    new_object, term = compute(
        False, True, corners[1], object_field, probe, left, right, arrived[1], acc, term, base
    )
    scale = 1.0 / math.sqrt(pos_dev * n_pos * n_obj)
    return new_object, summed(term, probe, n_pos, n_obj, scale)


def solution(mesh):
    placed = (
        P(None, "obj", "pos"),
        P(),
        P(("pos", "obj"), None, None),
        P(("pos", "obj")),
        P(("pos", "obj")),
        P(("pos", "obj")),
    )
    return jax.shard_map(
        shards, mesh=mesh, in_specs=placed, out_specs=(P(None, "obj", "pos"), P()), check_vma=False
    )
```

```python
import functools
import math

import jax
import jax.numpy as jnp
import numpy as np
from jax import lax
from jax.experimental import pallas as pl
from jax.experimental.pallas import tpu as pltpu
from jax.sharding import PartitionSpec as P

SIZE = 256
CAPACITY = 2
LANES = 128
F32 = jnp.float32
BF16 = jnp.bfloat16


def dft_blocks():
    index = np.arange(SIZE, dtype=np.int64)
    product = (index[:, None] * index[None, :]) % SIZE
    angle = product.astype(np.float32) * np.float32(2.0 * math.pi / SIZE)
    scale = 1.0 / math.sqrt(SIZE)
    real = (np.cos(angle.astype(np.float64)) * scale).astype(np.float32)
    imag = (-np.sin(angle.astype(np.float64)) * scale).astype(np.float32)
    real = jnp.asarray(real).astype(BF16)
    imag = jnp.asarray(imag).astype(BF16)
    top = jnp.concatenate([real, -imag], axis=1)
    bottom = jnp.concatenate([imag, real], axis=1)
    left = jnp.concatenate([top, bottom], axis=0)
    top = jnp.concatenate([real, imag], axis=1)
    bottom = jnp.concatenate([-imag, real], axis=1)
    return left, jnp.concatenate([top, bottom], axis=0)


STRIP = 32


def extract(meta_row, meta_col, tile, probe, window, psi, j):
    lane = lax.broadcasted_iota(jnp.int32, (STRIP, LANES), 1)
    first = lane < LANES - meta_col
    shift = lax.rem(LANES - meta_col, LANES)
    for s in range(0, SIZE, STRIP):
        parts = []
        for p in range(2):
            t = [
                pltpu.roll(tile[p, k, pl.ds(meta_row + s, STRIP), :], shift, 1)
                for k in range(3)
            ]
            parts.append([jnp.where(first, t[k], t[k + 1]) for k in range(2)])
        for k in range(2):
            cols = slice(k * LANES, (k + 1) * LANES)
            x_re, x_im = parts[0][k], parts[1][k]
            window[j, 0, s : s + STRIP, cols] = x_re
            window[j, 1, s : s + STRIP, cols] = x_im
            p_re = probe[0, s : s + STRIP, cols]
            p_im = probe[1, s : s + STRIP, cols]
            out = slice(j * SIZE + k * LANES, j * SIZE + (k + 1) * LANES)
            psi[s : s + STRIP, out] = (p_re * x_re - p_im * x_im).astype(BF16)
            psi[SIZE + s : SIZE + s + STRIP, out] = (p_re * x_im + p_im * x_re).astype(BF16)


def turn(value, out):
    for j in range(2):
        for part in range(2):
            out[j * SIZE : (j + 1) * SIZE, part * SIZE : (part + 1) * SIZE] = value[
                part * SIZE : (part + 1) * SIZE, j * SIZE : (j + 1) * SIZE
            ].astype(BF16)


def modulus(wave, amp, diff, j):
    for s in range(0, SIZE, STRIP):
        rows = slice(j * SIZE + s, j * SIZE + s + STRIP)
        w_re = wave[rows, 0:SIZE]
        w_im = wave[rows, SIZE : 2 * SIZE]
        a = amp[j, s : s + STRIP, :].astype(F32)
        power = w_re * w_re + w_im * w_im
        factor = 1.0 - a * lax.rsqrt(jnp.maximum(power, 0.25))
        cols = slice(j * SIZE, (j + 1) * SIZE)
        diff[s : s + STRIP, cols] = (w_re * factor).astype(BF16)
        diff[SIZE + s : SIZE + s + STRIP, cols] = (w_im * factor).astype(BF16)


def gradients(meta_col, chi, probe, window, spread, term, j):
    lane = lax.broadcasted_iota(jnp.int32, (STRIP, LANES), 1)
    later = lane >= meta_col
    shift = lax.rem(meta_col, LANES)
    zero = jnp.zeros((STRIP, LANES), F32)
    for s in range(0, SIZE, STRIP):
        rows = slice(j * SIZE + s, j * SIZE + s + STRIP)
        turned = [[], []]
        for k in range(2):
            cols = slice(k * LANES, (k + 1) * LANES)
            c_re = chi[rows, k * LANES : (k + 1) * LANES]
            c_im = chi[rows, SIZE + k * LANES : SIZE + (k + 1) * LANES]
            x_re = window[j, 0, s : s + STRIP, cols]
            x_im = window[j, 1, s : s + STRIP, cols]
            term[0, s : s + STRIP, cols] += x_re * c_re + x_im * c_im
            term[1, s : s + STRIP, cols] += x_re * c_im - x_im * c_re
            p_re = probe[0, s : s + STRIP, cols]
            p_im = probe[1, s : s + STRIP, cols]
            g_re = (p_re * c_re + p_im * c_im).astype(BF16).astype(F32)
            g_im = (p_re * c_im - p_im * c_re).astype(BF16).astype(F32)
            turned[0].append(pltpu.roll(g_re, shift, 1))
            turned[1].append(pltpu.roll(g_im, shift, 1))
        here = slice(SIZE + s, SIZE + s + STRIP)
        for p in range(2):
            low, high = turned[p]
            spread[j, p, 0, here, :] = jnp.where(later, low, zero)
            spread[j, p, 1, here, :] = jnp.where(later, high, low)
            spread[j, p, 2, here, :] = jnp.where(later, zero, high)


def accumulate(meta_row, spread, acc):
    starts = [SIZE - jnp.bitwise_and(meta_row[j], 2 * SIZE - 1) for j in range(2)]
    for p in range(2):
        for k in range(3):
            for s in range(0, 2 * SIZE, STRIP):
                acc[p, k, s : s + STRIP, :] += (
                    spread[0, p, k, pl.ds(starts[0] + s, STRIP), :]
                    + spread[1, p, k, pl.ds(starts[1] + s, STRIP), :]
                )


MESH = pl.DeviceIdType.MESH


def fused_kernel(
    n_pos, n_obj, scale,
    owner, rows, cols, amps, obj, probe, left, right,
    grad_out, probe_out,
    slots, landed, meta_out, meta_in, meta, tile, window, psi, half, wave, diff, chi, spread, acc,
    term, tiles, got_obj, part, got_pos, done,
    amp_send, amp_recv, meta_send, meta_recv, meta_sem, sum_send, sum_recv,
):
    me_p = lax.axis_index("pos")
    me_o = lax.axis_index("obj")
    side = math.isqrt(n_pos)
    peer_o = [lax.rem(me_o + d, n_obj) for d in range(1, n_obj)]

    def peer_at(s):
        x = lax.rem(me_p // side + s // side, side)
        y = lax.rem(me_p % side + s % side, side)
        return x * side + y

    peer_p = [peer_at(s) for s in range(1, n_pos)]

    barrier = pltpu.get_barrier_semaphore()
    for o in peer_o:
        pl.semaphore_signal(barrier, inc=1, device_id=(me_p, o), device_id_type=MESH)
    for p in peer_p:
        pl.semaphore_signal(barrier, inc=1, device_id=(p, me_o), device_id_type=MESH)
    pl.semaphore_wait(barrier, n_obj + n_pos - 2)

    def amp_copy(s):
        return pltpu.make_async_remote_copy(
            src_ref=slots.at[s], dst_ref=landed.at[s],
            send_sem=amp_send.at[s], recv_sem=amp_recv.at[s],
            device_id=(peer_at(s), me_o), device_id_type=MESH,
        )

    def meta_copy(s):
        return pltpu.make_async_remote_copy(
            src_ref=meta_out.at[s], dst_ref=meta_in.at[s],
            send_sem=meta_send.at[s], recv_sem=meta_recv.at[s],
            device_id=(peer_at(s), me_o), device_id_type=MESH,
        )

    lane = lax.broadcasted_iota(jnp.int32, (8, LANES), 1)

    def found(s):
        target = peer_at(s)
        first = jnp.int32(-1)
        second = jnp.int32(-1)
        for i in reversed(range(amps.shape[0])):
            hit = owner[i] == target
            second = jnp.where(hit, first, second)
            first = jnp.where(hit, i, first)
        return first, second

    def lay_out(s, out, corners):
        picked = found(s)
        values = jnp.zeros((8, LANES), jnp.int32)
        for k in range(CAPACITY):
            i = jnp.maximum(picked[k], 0)
            row = jnp.where(picked[k] < 0, 2 * SIZE, rows[i])
            values = jnp.where(lane == 2 * k, row, values)
            values = jnp.where(lane == 2 * k + 1, cols[i], values)
            out[s, k] = amps[i]
        corners[s] = values

    @pl.loop(1, n_pos)
    def _(s):
        lay_out(s, slots, meta_out)
        meta_copy(s).start()
        amp_copy(s).start()

    lay_out(0, landed, meta_in)
    for p in range(2):
        for k in range(3):
            block = slice(k * LANES, (k + 1) * LANES)
            tile[p, k, 0 : 2 * SIZE, :] = obj[p, :, block].astype(BF16).astype(F32)
            tile[p, k, 2 * SIZE : 3 * SIZE, :] = jnp.zeros((SIZE, LANES), F32)
            for j in range(2):
                spread[j, p, k, 0:SIZE, :] = jnp.zeros((SIZE, LANES), F32)
                spread[j, p, k, 2 * SIZE : 3 * SIZE, :] = jnp.zeros((SIZE, LANES), F32)
    acc[...] = jnp.zeros_like(acc)
    term[...] = jnp.zeros_like(term)

    @pl.loop(1, n_pos)
    def _(s):
        meta_copy(s).wait()

    to_scalars = pltpu.make_async_copy(meta_in, meta, meta_sem)
    to_scalars.start()
    to_scalars.wait()

    @pl.loop(0, n_pos)
    def _(s):
        @pl.when(s > 0)
        def _():
            amp_copy(s).wait()

        row = [meta[s, 0, 2 * j] for j in range(2)]
        col = [meta[s, 0, 2 * j + 1] for j in range(2)]
        amp = landed.at[s]
        for j in range(2):
            extract(row[j], col[j], tile, probe, window, psi, j)
        turn(jnp.dot(left[...], psi[...], preferred_element_type=F32), half)
        wave[...] = jnp.dot(half[...], right[...], preferred_element_type=F32)
        for j in range(2):
            modulus(wave, amp, diff, j)
        turn(jnp.dot(right[...], diff[...], preferred_element_type=F32), half)
        chi[...] = jnp.dot(half[...], left[...], preferred_element_type=F32)
        for j in range(2):
            gradients(col[j], chi, probe, window, spread, term, j)
        accumulate(row, spread, acc)

    for p in range(2):
        for k in range(3):
            grad_out[p, :, k * LANES : (k + 1) * LANES] = acc[p, k]

    for plane in range(2):
        for i in range(SIZE // 8):
            for k in range(2):
                tiles[(plane * (SIZE // 8) + i) * 2 + k] = term[
                    plane, 8 * i : 8 * i + 8, k * LANES : (k + 1) * LANES
                ]

    def over_obj(base, source_of, target_of):
        return [
            pltpu.make_async_remote_copy(
                src_ref=source_of(d, o), dst_ref=target_of(d, o),
                send_sem=sum_send.at[base + d], recv_sem=sum_recv.at[base + d],
                device_id=(me_p, o), device_id_type=MESH,
            )
            for d, o in enumerate(peer_o)
        ]

    def over_pos(base, source_of, target_of):
        return [
            pltpu.make_async_remote_copy(
                src_ref=source_of(d, p), dst_ref=target_of(d, p),
                send_sem=sum_send.at[base + d], recv_sem=sum_recv.at[base + d],
                device_id=(p, me_o), device_id_type=MESH,
            )
            for d, p in enumerate(peer_p)
        ]

    step = n_obj - 1 + n_pos - 1
    copies = over_obj(0, lambda d, o: tiles.at[pl.ds(o * n_pos, n_pos)], lambda d, o: got_obj.at[d])
    for c in copies:
        c.start()
    for c in copies:
        c.wait_recv()
    total = tiles[pl.ds(me_o * n_pos, n_pos)]
    for d in range(n_obj - 1):
        total += got_obj[d]
    part[...] = total
    second = over_pos(n_obj - 1, lambda d, p: part.at[p], lambda d, p: got_pos.at[d])
    for c in second:
        c.start()
    for c in second:
        c.wait_recv()
    total = part[me_p]
    for d in range(n_pos - 1):
        total += got_pos[d]
    mine = me_o * n_pos + me_p
    done[mine] = total
    third = over_pos(step, lambda d, p: done.at[mine], lambda d, p: done.at[mine])
    for c in third:
        c.start()
    for c in third:
        c.wait_recv()
    block = pl.ds(me_o * n_pos, n_pos)
    fourth = over_obj(step + n_pos - 1, lambda d, o: done.at[block], lambda d, o: done.at[block])
    for c in fourth:
        c.start()
    for c in fourth:
        c.wait_recv()
    for c in copies + second + third + fourth:
        c.wait_send()
    for plane in range(2):
        for i in range(SIZE // 8):
            for k in range(2):
                here, block = slice(8 * i, 8 * i + 8), slice(k * LANES, (k + 1) * LANES)
                probe_out[plane, here, block] = probe[plane, here, block] - scale * done[
                    (plane * (SIZE // 8) + i) * 2 + k
                ]


def fused(owner, rows, cols, amps, obj, probe, left, right, n_pos, n_obj, scale):
    smem = pl.BlockSpec(memory_space=pltpu.SMEM)
    vmem = pl.BlockSpec(memory_space=pltpu.VMEM)
    count = 2 * (n_pos + n_obj - 2)
    total = n_pos * n_obj
    double = (2 * SIZE, 2 * SIZE)
    dma = pltpu.SemaphoreType.DMA
    return pl.pallas_call(
        functools.partial(fused_kernel, n_pos, n_obj, scale),
        out_shape=(
            jax.ShapeDtypeStruct(obj.shape, F32),
            jax.ShapeDtypeStruct(probe.shape, F32),
        ),
        in_specs=[smem, smem, smem, vmem, vmem, vmem, vmem, vmem],
        out_specs=(vmem, vmem),
        scratch_shapes=[
            pltpu.VMEM((n_pos, CAPACITY, SIZE, SIZE), BF16),
            pltpu.VMEM((n_pos, CAPACITY, SIZE, SIZE), BF16),
            pltpu.VMEM((n_pos, 8, LANES), jnp.int32),
            pltpu.VMEM((n_pos, 8, LANES), jnp.int32),
            pltpu.SMEM((n_pos, 8, LANES), jnp.int32),
            pltpu.VMEM((2, 3, 3 * SIZE, LANES), F32),
            pltpu.VMEM((2, 2, SIZE, SIZE), F32),
            pltpu.VMEM(double, BF16),
            pltpu.VMEM(double, BF16),
            pltpu.VMEM(double, F32),
            pltpu.VMEM(double, BF16),
            pltpu.VMEM(double, F32),
            pltpu.VMEM((2, 2, 3, 3 * SIZE, LANES), F32),
            pltpu.VMEM((2, 3, 2 * SIZE, LANES), F32),
            pltpu.VMEM((2, SIZE, SIZE), F32),
            pltpu.VMEM((total, 8, LANES), F32),
            pltpu.VMEM((n_obj - 1, n_pos, 8, LANES), F32),
            pltpu.VMEM((n_pos, 8, LANES), F32),
            pltpu.VMEM((n_pos - 1, 8, LANES), F32),
            pltpu.VMEM((total, 8, LANES), F32),
            dma((n_pos,)), dma((n_pos,)), dma((n_pos,)), dma((n_pos,)), dma,
            dma((count,)), dma((count,)),
        ],
        compiler_params=pltpu.CompilerParams(
            collective_id=1, has_side_effects=True, vmem_limit_bytes=56 << 20
        ),
        cost_estimate=pl.CostEstimate(
            flops=2 * n_pos * 32 * SIZE**3, bytes_accessed=16 << 20, transcendentals=0
        ),
        name="fused",
    )(owner, rows, cols, amps, obj, probe, left, right)


def exchanged(block, axis, dim):
    count = lax.axis_size(axis)
    forward = [(i, (i + 1) % count) for i in range(count)]
    backward = [(target, source) for source, target in forward]
    size = block.shape[dim]
    low = lax.ppermute(lax.slice_in_dim(block, size - 1, size, axis=dim), axis, forward)
    high = lax.ppermute(lax.slice_in_dim(block, 0, 1, axis=dim), axis, backward)
    return jnp.concatenate([low, block, high], axis=dim)


def shards(object_field, probe, amplitude, row_offset, col_offset, owner):
    n_pos = lax.axis_size("pos")
    n_obj = lax.axis_size("obj")
    pos_dev = amplitude.shape[0]
    left, right = dft_blocks()
    scale = 1.0 / math.sqrt(pos_dev * n_pos * n_obj)
    tall = exchanged(object_field, "obj", 1)
    wide = exchanged(object_field, "pos", 2)
    smooth = 4.0 * object_field - tall[:, :-2] - tall[:, 2:] - wide[:, :, :-2] - wide[:, :, 2:]
    grad, new_probe = fused(
        owner, row_offset, col_offset, amplitude, object_field, probe, left, right,
        n_pos, n_obj, scale,
    )
    return object_field - 0.25 * (grad + 0.5 * smooth), new_probe


def solution(mesh):
    placed = (
        P(None, "obj", "pos"),
        P(),
        P(("pos", "obj"), None, None),
        P(("pos", "obj")),
        P(("pos", "obj")),
        P(("pos", "obj")),
    )
    return jax.shard_map(
        shards, mesh=mesh, in_specs=placed, out_specs=(P(None, "obj", "pos"), P()), check_vma=False
    )
```

```python
import functools
import math

import jax
import jax.numpy as jnp
import numpy as np
from jax import lax
from jax.experimental import pallas as pl
from jax.experimental.pallas import tpu as pltpu
from jax.sharding import PartitionSpec as P

SIZE = 256
CAPACITY = 2
LANES = 128
F32 = jnp.float32
BF16 = jnp.bfloat16


def dft_blocks():
    index = np.arange(SIZE, dtype=np.int64)
    product = (index[:, None] * index[None, :]) % SIZE
    angle = product.astype(np.float32) * np.float32(2.0 * math.pi / SIZE)
    scale = 1.0 / math.sqrt(SIZE)
    real = (np.cos(angle.astype(np.float64)) * scale).astype(np.float32)
    imag = (-np.sin(angle.astype(np.float64)) * scale).astype(np.float32)
    real = jnp.asarray(real).astype(BF16)
    imag = jnp.asarray(imag).astype(BF16)
    top = jnp.concatenate([real, -imag], axis=1)
    bottom = jnp.concatenate([imag, real], axis=1)
    left = jnp.concatenate([top, bottom], axis=0)
    top = jnp.concatenate([real, imag], axis=1)
    bottom = jnp.concatenate([-imag, real], axis=1)
    return left, jnp.concatenate([top, bottom], axis=0)


STRIP = 32


def extract(meta_row, meta_col, tile, probe, window, psi, j):
    lane = lax.broadcasted_iota(jnp.int32, (STRIP, LANES), 1)
    first = lane < LANES - meta_col
    shift = lax.rem(LANES - meta_col, LANES)
    for s in range(0, SIZE, STRIP):
        parts = []
        for p in range(2):
            t = [
                pltpu.roll(tile[p, k, pl.ds(meta_row + s, STRIP), :], shift, 1)
                for k in range(3)
            ]
            parts.append([jnp.where(first, t[k], t[k + 1]) for k in range(2)])
        for k in range(2):
            cols = slice(k * LANES, (k + 1) * LANES)
            x_re, x_im = parts[0][k], parts[1][k]
            window[j, 0, s : s + STRIP, cols] = x_re
            window[j, 1, s : s + STRIP, cols] = x_im
            p_re = probe[0, s : s + STRIP, cols]
            p_im = probe[1, s : s + STRIP, cols]
            out = slice(j * SIZE + k * LANES, j * SIZE + (k + 1) * LANES)
            psi[s : s + STRIP, out] = (p_re * x_re - p_im * x_im).astype(BF16)
            psi[SIZE + s : SIZE + s + STRIP, out] = (p_re * x_im + p_im * x_re).astype(BF16)


def turn(value, out):
    for j in range(2):
        for part in range(2):
            out[j * SIZE : (j + 1) * SIZE, part * SIZE : (part + 1) * SIZE] = value[
                part * SIZE : (part + 1) * SIZE, j * SIZE : (j + 1) * SIZE
            ].astype(BF16)


def modulus(wave, amp, diff, j):
    for s in range(0, SIZE, STRIP):
        rows = slice(j * SIZE + s, j * SIZE + s + STRIP)
        w_re = wave[rows, 0:SIZE]
        w_im = wave[rows, SIZE : 2 * SIZE]
        a = amp[j, s : s + STRIP, :].astype(F32)
        power = w_re * w_re + w_im * w_im
        factor = 1.0 - a * lax.rsqrt(jnp.maximum(power, 0.25))
        cols = slice(j * SIZE, (j + 1) * SIZE)
        diff[s : s + STRIP, cols] = (w_re * factor).astype(BF16)
        diff[SIZE + s : SIZE + s + STRIP, cols] = (w_im * factor).astype(BF16)


def gradients(meta_col, chi, probe, window, spread, term, j):
    lane = lax.broadcasted_iota(jnp.int32, (STRIP, LANES), 1)
    later = lane >= meta_col
    shift = lax.rem(meta_col, LANES)
    zero = jnp.zeros((STRIP, LANES), F32)
    for s in range(0, SIZE, STRIP):
        rows = slice(j * SIZE + s, j * SIZE + s + STRIP)
        turned = [[], []]
        for k in range(2):
            cols = slice(k * LANES, (k + 1) * LANES)
            c_re = chi[rows, k * LANES : (k + 1) * LANES]
            c_im = chi[rows, SIZE + k * LANES : SIZE + (k + 1) * LANES]
            x_re = window[j, 0, s : s + STRIP, cols]
            x_im = window[j, 1, s : s + STRIP, cols]
            term[0, s : s + STRIP, cols] += x_re * c_re + x_im * c_im
            term[1, s : s + STRIP, cols] += x_re * c_im - x_im * c_re
            p_re = probe[0, s : s + STRIP, cols]
            p_im = probe[1, s : s + STRIP, cols]
            g_re = (p_re * c_re + p_im * c_im).astype(BF16).astype(F32)
            g_im = (p_re * c_im - p_im * c_re).astype(BF16).astype(F32)
            turned[0].append(pltpu.roll(g_re, shift, 1))
            turned[1].append(pltpu.roll(g_im, shift, 1))
        here = slice(SIZE + s, SIZE + s + STRIP)
        for p in range(2):
            low, high = turned[p]
            spread[j, p, 0, here, :] = jnp.where(later, low, zero)
            spread[j, p, 1, here, :] = jnp.where(later, high, low)
            spread[j, p, 2, here, :] = jnp.where(later, zero, high)


def accumulate(meta_row, spread, acc):
    starts = [SIZE - jnp.bitwise_and(meta_row[j], 2 * SIZE - 1) for j in range(2)]
    for p in range(2):
        for k in range(3):
            for s in range(0, 2 * SIZE, STRIP):
                acc[p, k, s : s + STRIP, :] += (
                    spread[0, p, k, pl.ds(starts[0] + s, STRIP), :]
                    + spread[1, p, k, pl.ds(starts[1] + s, STRIP), :]
                )


MESH = pl.DeviceIdType.MESH


AHEAD = 6


def message_order(side):
    pending = [(x, y) for x in range(side) for y in range(side)]
    hops = lambda d: min(d, side - d)

    def rank(offset):
        x, y = offset
        first = min((x, y), ((side - x) % side, (side - y) % side))
        straight = 0 if 0 in offset else 1
        return (hops(x) + hops(y) - (hops(x) == hops(y)), straight, first)

    return sorted(pending, key=rank)


def fused_kernel(
    n_pos, n_obj, scale,
    owner, rows, cols, amps, obj, probe, left, right,
    object_out, probe_out,
    slots, landed, meta_out, meta_in, meta, tile, window, psi, half, wave, diff, chi, spread, acc,
    term, tiles, got_obj, part, got_pos, done, picked, ext, edge_out, edge_in, sides,
    amp_send, amp_recv, meta_send, meta_recv, meta_sem, sum_send, sum_recv, halo_send, halo_recv,
):
    me_p = lax.axis_index("pos")
    me_o = lax.axis_index("obj")
    side = math.isqrt(n_pos)
    peer_o = [lax.rem(me_o + d, n_obj) for d in range(1, n_obj)]

    order = message_order(side)

    def peer_at(s):
        if isinstance(s, int):
            dx, dy = order[s]
        else:
            dx = sum(jnp.where(s == i, d[0], 0) for i, d in enumerate(order) if d[0])
            dy = sum(jnp.where(s == i, d[1], 0) for i, d in enumerate(order) if d[1])
        x = lax.rem(me_p // side + dx, side)
        y = lax.rem(me_p % side + dy, side)
        return x * side + y

    peer_p = [peer_at(s) for s in range(1, n_pos)]

    barrier = pltpu.get_barrier_semaphore()
    for o in peer_o:
        pl.semaphore_signal(barrier, inc=1, device_id=(me_p, o), device_id_type=MESH)
    for p in peer_p:
        pl.semaphore_signal(barrier, inc=1, device_id=(p, me_o), device_id_type=MESH)
    pl.semaphore_wait(barrier, n_obj + n_pos - 2)

    def amp_copy(s):
        return pltpu.make_async_remote_copy(
            src_ref=slots.at[s], dst_ref=landed.at[s],
            send_sem=amp_send.at[s], recv_sem=amp_recv.at[s],
            device_id=(peer_at(s), me_o), device_id_type=MESH,
        )

    def meta_copy(s):
        return pltpu.make_async_remote_copy(
            src_ref=meta_out.at[s], dst_ref=meta_in.at[s],
            send_sem=meta_send.at[s], recv_sem=meta_recv.at[s],
            device_id=(peer_at(s), me_o), device_id_type=MESH,
        )

    lane = lax.broadcasted_iota(jnp.int32, (8, LANES), 1)

    def announce(s, corners):
        target = peer_at(s)
        first = jnp.int32(-1)
        second = jnp.int32(-1)
        for i in reversed(range(amps.shape[0])):
            hit = owner[i] == target
            second = jnp.where(hit, first, second)
            first = jnp.where(hit, i, first)
        values = jnp.zeros((8, LANES), jnp.int32)
        for k, found in enumerate((first, second)):
            i = jnp.maximum(found, 0)
            picked[s, k] = i
            row = jnp.where(found < 0, 2 * SIZE, rows[i])
            values = jnp.where(lane == 2 * k, row, values)
            values = jnp.where(lane == 2 * k + 1, cols[i], values)
        corners[s] = values

    def lay_out(s, out):
        for k in range(CAPACITY):
            out[s, k] = amps[picked[s, k]]

    @pl.loop(1, n_pos)
    def _(s):
        announce(s, meta_out)
        meta_copy(s).start()

    @pl.loop(1, 1 + AHEAD)
    def _(s):
        lay_out(s, slots)
        amp_copy(s).start()

    announce(0, meta_in)
    lay_out(0, landed)

    tall = 2 * SIZE
    next_p, last_p = lax.rem(me_p + 1, n_pos), lax.rem(me_p + n_pos - 1, n_pos)
    next_o, last_o = lax.rem(me_o + 1, n_obj), lax.rem(me_o + n_obj - 1, n_obj)

    def halo(i, source, target, device):
        return pltpu.make_async_remote_copy(
            src_ref=source, dst_ref=target, send_sem=halo_send.at[i], recv_sem=halo_recv.at[i],
            device_id=device, device_id_type=MESH,
        )

    for p in range(2):
        edge_out[0, p] = obj[p, :, 2 * LANES : 3 * LANES].T[LANES - 8 : LANES]
        edge_out[1, p] = obj[p, :, 0:LANES].T[0:8]
    halos = [
        halo(0, obj.at[:, pl.ds(tall - 8, 8), :], ext.at[:, pl.ds(0, 8), :], (me_p, next_o)),
        halo(1, obj.at[:, pl.ds(0, 8), :], ext.at[:, pl.ds(tall + 8, 8), :], (me_p, last_o)),
        halo(2, edge_out.at[0], edge_in.at[0], (next_p, me_o)),
        halo(3, edge_out.at[1], edge_in.at[1], (last_p, me_o)),
    ]
    for c in halos:
        c.start()
    for p in range(2):
        ext[p, 8 : tall + 8, :] = obj[p]
    for p in range(2):
        for k in range(3):
            block = slice(k * LANES, (k + 1) * LANES)
            tile[p, k, 0 : 2 * SIZE, :] = obj[p, :, block].astype(BF16).astype(F32)
            tile[p, k, 2 * SIZE : 3 * SIZE, :] = jnp.zeros((SIZE, LANES), F32)
            for j in range(2):
                spread[j, p, k, 0:SIZE, :] = jnp.zeros((SIZE, LANES), F32)
                spread[j, p, k, 2 * SIZE : 3 * SIZE, :] = jnp.zeros((SIZE, LANES), F32)
    acc[...] = jnp.zeros_like(acc)
    term[...] = jnp.zeros_like(term)

    @pl.loop(1, n_pos)
    def _(s):
        meta_copy(s).wait()

    to_scalars = pltpu.make_async_copy(meta_in, meta, meta_sem)
    to_scalars.start()
    to_scalars.wait()

    @pl.loop(0, n_pos)
    def _(s):
        @pl.when(s > 0)
        def _():
            amp_copy(s).wait_recv()

        @pl.when(s + AHEAD + 1 < n_pos)
        def _():
            lay_out(s + AHEAD + 1, slots)
            amp_copy(s + AHEAD + 1).start()

        row = [meta[s, 0, 2 * j] for j in range(2)]
        col = [meta[s, 0, 2 * j + 1] for j in range(2)]
        amp = landed.at[s]
        for j in range(2):
            extract(row[j], col[j], tile, probe, window, psi, j)
        turn(jnp.dot(left[...], psi[...], preferred_element_type=F32), half)
        wave[...] = jnp.dot(half[...], right[...], preferred_element_type=F32)
        for j in range(2):
            modulus(wave, amp, diff, j)
        turn(jnp.dot(right[...], diff[...], preferred_element_type=F32), half)
        chi[...] = jnp.dot(half[...], left[...], preferred_element_type=F32)
        for j in range(2):
            gradients(col[j], chi, probe, window, spread, term, j)
        accumulate(row, spread, acc)

    for plane in range(2):
        for i in range(SIZE // 8):
            for k in range(2):
                tiles[(plane * (SIZE // 8) + i) * 2 + k] = term[
                    plane, 8 * i : 8 * i + 8, k * LANES : (k + 1) * LANES
                ]

    def over_obj(base, source_of, target_of):
        return [
            pltpu.make_async_remote_copy(
                src_ref=source_of(d, o), dst_ref=target_of(d, o),
                send_sem=sum_send.at[base + d], recv_sem=sum_recv.at[base + d],
                device_id=(me_p, o), device_id_type=MESH,
            )
            for d, o in enumerate(peer_o)
        ]

    def over_pos(base, source_of, target_of):
        return [
            pltpu.make_async_remote_copy(
                src_ref=source_of(d, p), dst_ref=target_of(d, p),
                send_sem=sum_send.at[base + d], recv_sem=sum_recv.at[base + d],
                device_id=(p, me_o), device_id_type=MESH,
            )
            for d, p in enumerate(peer_p)
        ]

    step = n_obj - 1 + n_pos - 1
    copies = over_obj(0, lambda d, o: tiles.at[pl.ds(o * n_pos, n_pos)], lambda d, o: got_obj.at[d])
    for c in copies:
        c.start()
    for c in halos:
        c.wait()
    middle = jnp.zeros((LANES - 16, tall), F32)
    for p in range(2):
        sides[p] = jnp.concatenate([edge_in[1, p], middle, edge_in[0, p]], axis=0).T
    lanes = lax.broadcasted_iota(jnp.int32, (STRIP, LANES), 1)
    for p in range(2):
        for s in range(0, tall, STRIP):
            here = [ext[p, 8 + s : 8 + s + STRIP, k * LANES : (k + 1) * LANES] for k in range(3)]
            here.append(sides[p, s : s + STRIP, :])
            right_of = [pltpu.roll(t, LANES - 1, 1) for t in here]
            left_of = [pltpu.roll(t, 1, 1) for t in here]
            for k in range(3):
                block = slice(k * LANES, (k + 1) * LANES)
                around = ext[p, 7 + s : 7 + s + STRIP, block] + ext[p, 9 + s : 9 + s + STRIP, block]
                around += jnp.where(lanes == 0, left_of[k - 1], left_of[k])
                around += jnp.where(lanes == LANES - 1, right_of[k + 1], right_of[k])
                object_out[p, s : s + STRIP, block] = (
                    0.5 * here[k] + 0.125 * around - 0.25 * acc[p, k, s : s + STRIP, :]
                )

    @pl.loop(1, n_pos)
    def _(s):
        amp_copy(s).wait_send()

    for c in copies:
        c.wait_recv()
    total = tiles[pl.ds(me_o * n_pos, n_pos)]
    for d in range(n_obj - 1):
        total += got_obj[d]
    part[...] = total
    second = over_pos(n_obj - 1, lambda d, p: part.at[p], lambda d, p: got_pos.at[d])
    for c in second:
        c.start()
    for c in second:
        c.wait_recv()
    total = part[me_p]
    for d in range(n_pos - 1):
        total += got_pos[d]
    mine = me_o * n_pos + me_p
    done[mine] = total
    third = over_pos(step, lambda d, p: done.at[mine], lambda d, p: done.at[mine])
    for c in third:
        c.start()
    for c in third:
        c.wait_recv()
    block = pl.ds(me_o * n_pos, n_pos)
    fourth = over_obj(step + n_pos - 1, lambda d, o: done.at[block], lambda d, o: done.at[block])
    for c in fourth:
        c.start()
    for c in fourth:
        c.wait_recv()
    for c in copies + second + third + fourth:
        c.wait_send()
    for plane in range(2):
        for i in range(SIZE // 8):
            for k in range(2):
                here, block = slice(8 * i, 8 * i + 8), slice(k * LANES, (k + 1) * LANES)
                probe_out[plane, here, block] = probe[plane, here, block] - scale * done[
                    (plane * (SIZE // 8) + i) * 2 + k
                ]


def fused(owner, rows, cols, amps, obj, probe, left, right, n_pos, n_obj, scale):
    smem = pl.BlockSpec(memory_space=pltpu.SMEM)
    vmem = pl.BlockSpec(memory_space=pltpu.VMEM)
    count = 2 * (n_pos + n_obj - 2)
    total = n_pos * n_obj
    double = (2 * SIZE, 2 * SIZE)
    dma = pltpu.SemaphoreType.DMA
    return pl.pallas_call(
        functools.partial(fused_kernel, n_pos, n_obj, scale),
        out_shape=(
            jax.ShapeDtypeStruct(obj.shape, F32),
            jax.ShapeDtypeStruct(probe.shape, F32),
        ),
        in_specs=[smem, smem, smem, vmem, vmem, vmem, vmem, vmem],
        out_specs=(vmem, vmem),
        scratch_shapes=[
            pltpu.VMEM((n_pos, CAPACITY, SIZE, SIZE), BF16),
            pltpu.VMEM((n_pos, CAPACITY, SIZE, SIZE), BF16),
            pltpu.VMEM((n_pos, 8, LANES), jnp.int32),
            pltpu.VMEM((n_pos, 8, LANES), jnp.int32),
            pltpu.SMEM((n_pos, 8, LANES), jnp.int32),
            pltpu.VMEM((2, 3, 3 * SIZE, LANES), F32),
            pltpu.VMEM((2, 2, SIZE, SIZE), F32),
            pltpu.VMEM(double, BF16),
            pltpu.VMEM(double, BF16),
            pltpu.VMEM(double, F32),
            pltpu.VMEM(double, BF16),
            pltpu.VMEM(double, F32),
            pltpu.VMEM((2, 2, 3, 3 * SIZE, LANES), F32),
            pltpu.VMEM((2, 3, 2 * SIZE, LANES), F32),
            pltpu.VMEM((2, SIZE, SIZE), F32),
            pltpu.VMEM((total, 8, LANES), F32),
            pltpu.VMEM((n_obj - 1, n_pos, 8, LANES), F32),
            pltpu.VMEM((n_pos, 8, LANES), F32),
            pltpu.VMEM((n_pos - 1, 8, LANES), F32),
            pltpu.VMEM((total, 8, LANES), F32),
            pltpu.SMEM((n_pos, CAPACITY), jnp.int32),
            pltpu.VMEM((2, 2 * SIZE + 16, 3 * LANES), F32),
            pltpu.VMEM((2, 2, 8, 2 * SIZE), F32),
            pltpu.VMEM((2, 2, 8, 2 * SIZE), F32),
            pltpu.VMEM((2, 2 * SIZE, LANES), F32),
            dma((n_pos,)), dma((n_pos,)), dma((n_pos,)), dma((n_pos,)), dma,
            dma((count,)), dma((count,)), dma((4,)), dma((4,)),
        ],
        compiler_params=pltpu.CompilerParams(
            collective_id=1, has_side_effects=True, vmem_limit_bytes=56 << 20
        ),
        cost_estimate=pl.CostEstimate(
            flops=2 * n_pos * 32 * SIZE**3, bytes_accessed=16 << 20, transcendentals=0
        ),
        name="fused",
    )(owner, rows, cols, amps, obj, probe, left, right)


def shards(object_field, probe, amplitude, row_offset, col_offset, owner):
    n_pos = lax.axis_size("pos")
    n_obj = lax.axis_size("obj")
    pos_dev = amplitude.shape[0]
    left, right = dft_blocks()
    scale = 1.0 / math.sqrt(pos_dev * n_pos * n_obj)
    return fused(
        owner, row_offset, col_offset, amplitude, object_field, probe, left, right,
        n_pos, n_obj, scale,
    )


def solution(mesh):
    placed = (
        P(None, "obj", "pos"),
        P(),
        P(("pos", "obj"), None, None),
        P(("pos", "obj")),
        P(("pos", "obj")),
        P(("pos", "obj")),
    )
    return jax.shard_map(
        shards, mesh=mesh, in_specs=placed, out_specs=(P(None, "obj", "pos"), P()), check_vma=False
    )
```

```python
import functools
import math

import jax
import jax.numpy as jnp
import numpy as np
from jax import lax
from jax.experimental import pallas as pl
from jax.experimental.pallas import tpu as pltpu
from jax.sharding import PartitionSpec as P

SIZE = 256
CAPACITY = 2
LANES = 128
F32 = jnp.float32
BF16 = jnp.bfloat16


def dft_blocks():
    index = np.arange(SIZE, dtype=np.int64)
    product = (index[:, None] * index[None, :]) % SIZE
    angle = product.astype(np.float32) * np.float32(2.0 * math.pi / SIZE)
    scale = 1.0 / math.sqrt(SIZE)
    real = (np.cos(angle.astype(np.float64)) * scale).astype(np.float32)
    imag = (-np.sin(angle.astype(np.float64)) * scale).astype(np.float32)
    real = jnp.asarray(real).astype(BF16)
    imag = jnp.asarray(imag).astype(BF16)
    top = jnp.concatenate([real, -imag], axis=1)
    bottom = jnp.concatenate([imag, real], axis=1)
    left = jnp.concatenate([top, bottom], axis=0)
    top = jnp.concatenate([real, imag], axis=1)
    bottom = jnp.concatenate([-imag, real], axis=1)
    return left, jnp.concatenate([top, bottom], axis=0)


STRIP = 32


def extract(meta_row, meta_col, tile, probe, window, psi, j):
    lane = lax.broadcasted_iota(jnp.int32, (STRIP, LANES), 1)
    first = lane < LANES - meta_col
    shift = lax.rem(LANES - meta_col, LANES)
    for s in range(0, SIZE, STRIP):
        parts = []
        for p in range(2):
            t = [
                pltpu.roll(tile[p, k, pl.ds(meta_row + s, STRIP), :], shift, 1)
                for k in range(3)
            ]
            parts.append([jnp.where(first, t[k], t[k + 1]) for k in range(2)])
        for k in range(2):
            cols = slice(k * LANES, (k + 1) * LANES)
            x_re, x_im = parts[0][k], parts[1][k]
            window[j, 0, s : s + STRIP, cols] = x_re
            window[j, 1, s : s + STRIP, cols] = x_im
            p_re = probe[0, s : s + STRIP, cols]
            p_im = probe[1, s : s + STRIP, cols]
            out = slice(j * SIZE + k * LANES, j * SIZE + (k + 1) * LANES)
            psi[s : s + STRIP, out] = (p_re * x_re - p_im * x_im).astype(BF16)
            psi[SIZE + s : SIZE + s + STRIP, out] = (p_re * x_im + p_im * x_re).astype(BF16)


def turn(value, out):
    for j in range(2):
        for part in range(2):
            out[j * SIZE : (j + 1) * SIZE, part * SIZE : (part + 1) * SIZE] = value[
                part * SIZE : (part + 1) * SIZE, j * SIZE : (j + 1) * SIZE
            ].astype(BF16)


def modulus(wave, amp, diff, j):
    for s in range(0, SIZE, STRIP):
        rows = slice(j * SIZE + s, j * SIZE + s + STRIP)
        w_re = wave[rows, 0:SIZE]
        w_im = wave[rows, SIZE : 2 * SIZE]
        a = amp[j, s : s + STRIP, :].astype(F32)
        power = w_re * w_re + w_im * w_im
        factor = 1.0 - a * lax.rsqrt(jnp.maximum(power, 0.25))
        cols = slice(j * SIZE, (j + 1) * SIZE)
        diff[s : s + STRIP, cols] = (w_re * factor).astype(BF16)
        diff[SIZE + s : SIZE + s + STRIP, cols] = (w_im * factor).astype(BF16)


def gradients(meta_col, chi, probe, window, spread, term, j):
    lane = lax.broadcasted_iota(jnp.int32, (STRIP, LANES), 1)
    later = lane >= meta_col
    shift = lax.rem(meta_col, LANES)
    zero = jnp.zeros((STRIP, LANES), F32)
    for s in range(0, SIZE, STRIP):
        rows = slice(j * SIZE + s, j * SIZE + s + STRIP)
        turned = [[], []]
        for k in range(2):
            cols = slice(k * LANES, (k + 1) * LANES)
            c_re = chi[rows, k * LANES : (k + 1) * LANES]
            c_im = chi[rows, SIZE + k * LANES : SIZE + (k + 1) * LANES]
            x_re = window[j, 0, s : s + STRIP, cols]
            x_im = window[j, 1, s : s + STRIP, cols]
            term[0, s : s + STRIP, cols] += x_re * c_re + x_im * c_im
            term[1, s : s + STRIP, cols] += x_re * c_im - x_im * c_re
            p_re = probe[0, s : s + STRIP, cols]
            p_im = probe[1, s : s + STRIP, cols]
            g_re = (p_re * c_re + p_im * c_im).astype(BF16).astype(F32)
            g_im = (p_re * c_im - p_im * c_re).astype(BF16).astype(F32)
            turned[0].append(pltpu.roll(g_re, shift, 1))
            turned[1].append(pltpu.roll(g_im, shift, 1))
        here = slice(SIZE + s, SIZE + s + STRIP)
        for p in range(2):
            low, high = turned[p]
            spread[j, p, 0, here, :] = jnp.where(later, low, zero)
            spread[j, p, 1, here, :] = jnp.where(later, high, low)
            spread[j, p, 2, here, :] = jnp.where(later, zero, high)


def accumulate(meta_row, spread, acc):
    starts = [SIZE - jnp.bitwise_and(meta_row[j], 2 * SIZE - 1) for j in range(2)]
    for p in range(2):
        for k in range(3):
            for s in range(0, 2 * SIZE, STRIP):
                acc[p, k, s : s + STRIP, :] += (
                    spread[0, p, k, pl.ds(starts[0] + s, STRIP), :]
                    + spread[1, p, k, pl.ds(starts[1] + s, STRIP), :]
                )


MESH = pl.DeviceIdType.MESH


ORDER = (
    (0, 0),
    (0, 1), (0, 3), (1, 0), (3, 0),
    (1, 2), (3, 2), (2, 0),
    (2, 1), (2, 3), (0, 2),
    (1, 1), (3, 3),
    (1, 3), (3, 1),
    (2, 2),
)
AT_ONCE = 4
STARTED = (7, 7, 7, 10, 10, 12, 12, 14, 14, 15, 15, 15, 15, 15, 15, 15)


def chosen(s, table):
    return sum(jnp.where(s == i, v, 0) for i, v in enumerate(table) if v)


def fused_kernel(
    n_pos, n_obj, scale,
    owner, rows, cols, amps_hbm, obj_hbm, probe_hbm, left_hbm, right_hbm,
    object_hbm, probe_out,
    amps, probe, left, right, object_out,
    slots, landed, meta_out, meta_in, meta, tile, window, psi, half, wave, diff, chi, spread, acc,
    term, exact, rounded, got_a, got_b, all_a, all_b, done, picked, ext, edge_out, edge_in, sides,
    load_sem, amp_send, amp_recv, meta_send, meta_recv, meta_sem, sum_send, sum_recv,
    halo_send, halo_recv, out_sem,
):
    tall = 2 * SIZE
    inner = ext.at[:, pl.ds(8, tall), :]
    loads = [
        pltpu.make_async_copy(source, target, load_sem.at[i])
        for i, (source, target) in enumerate(
            ((amps_hbm, amps), (obj_hbm, inner), (probe_hbm, probe), (left_hbm, left), (right_hbm, right))
        )
    ]
    for c in loads:
        c.start()
    me_p = lax.axis_index("pos")
    me_o = lax.axis_index("obj")
    side = math.isqrt(n_pos)
    peer_o = [lax.rem(me_o + d, n_obj) for d in range(1, n_obj)]


    def peer_at(s):
        if isinstance(s, int):
            dx, dy = ORDER[s]
        else:
            dx = chosen(s, [d[0] for d in ORDER])
            dy = chosen(s, [d[1] for d in ORDER])
        x = lax.rem(me_p // side + dx, side)
        y = lax.rem(me_p % side + dy, side)
        return x * side + y

    peer_p = [peer_at(s) for s in range(1, n_pos)]

    barrier = pltpu.get_barrier_semaphore()
    for o in peer_o:
        pl.semaphore_signal(barrier, inc=1, device_id=(me_p, o), device_id_type=MESH)
    for p in peer_p:
        pl.semaphore_signal(barrier, inc=1, device_id=(p, me_o), device_id_type=MESH)
    pl.semaphore_wait(barrier, n_obj + n_pos - 2)

    def amp_copy(s):
        return pltpu.make_async_remote_copy(
            src_ref=slots.at[s], dst_ref=landed.at[s],
            send_sem=amp_send.at[s], recv_sem=amp_recv.at[s],
            device_id=(peer_at(s), me_o), device_id_type=MESH,
        )

    def meta_copy(s):
        return pltpu.make_async_remote_copy(
            src_ref=meta_out.at[s], dst_ref=meta_in.at[s],
            send_sem=meta_send.at[s], recv_sem=meta_recv.at[s],
            device_id=(peer_at(s), me_o), device_id_type=MESH,
        )

    lane = lax.broadcasted_iota(jnp.int32, (8, LANES), 1)

    def announce(s, corners):
        target = peer_at(s)
        first = jnp.int32(-1)
        second = jnp.int32(-1)
        for i in reversed(range(amps.shape[0])):
            hit = owner[i] == target
            second = jnp.where(hit, first, second)
            first = jnp.where(hit, i, first)
        values = jnp.zeros((8, LANES), jnp.int32)
        for k, found in enumerate((first, second)):
            i = jnp.maximum(found, 0)
            picked[s, k] = i
            row = jnp.where(found < 0, 2 * SIZE, rows[i])
            values = jnp.where(lane == 2 * k, row, values)
            values = jnp.where(lane == 2 * k + 1, cols[i], values)
        corners[s] = values

    def lay_out(s, out):
        for k in range(CAPACITY):
            out[s, k] = amps[picked[s, k]]

    def send(s):
        lay_out(s, slots)
        amp_copy(s).start()

    loads[0].wait()

    @pl.loop(1, 1 + AT_ONCE)
    def _(s):
        announce(s, meta_out)
        meta_copy(s).start()
        send(s)

    @pl.loop(1 + AT_ONCE, n_pos)
    def _(s):
        announce(s, meta_out)
        meta_copy(s).start()

    announce(0, meta_in)
    lay_out(0, landed)
    loads[1].wait()

    next_p, last_p = lax.rem(me_p + 1, n_pos), lax.rem(me_p + n_pos - 1, n_pos)
    next_o, last_o = lax.rem(me_o + 1, n_obj), lax.rem(me_o + n_obj - 1, n_obj)

    def halo(i, source, target, device):
        return pltpu.make_async_remote_copy(
            src_ref=source, dst_ref=target, send_sem=halo_send.at[i], recv_sem=halo_recv.at[i],
            device_id=device, device_id_type=MESH,
        )

    for p in range(2):
        edge_out[0, p] = ext[p, 8 : tall + 8, 2 * LANES : 3 * LANES].T[LANES - 8 : LANES]
        edge_out[1, p] = ext[p, 8 : tall + 8, 0:LANES].T[0:8]
    halos = [
        halo(0, ext.at[:, pl.ds(tall, 8), :], ext.at[:, pl.ds(0, 8), :], (me_p, next_o)),
        halo(1, ext.at[:, pl.ds(8, 8), :], ext.at[:, pl.ds(tall + 8, 8), :], (me_p, last_o)),
        halo(2, edge_out.at[0], edge_in.at[0], (next_p, me_o)),
        halo(3, edge_out.at[1], edge_in.at[1], (last_p, me_o)),
    ]
    for c in halos:
        c.start()
    for p in range(2):
        for k in range(3):
            block = slice(k * LANES, (k + 1) * LANES)
            tile[p, k, 0 : 2 * SIZE, :] = ext[p, 8 : tall + 8, block].astype(BF16).astype(F32)
            tile[p, k, 2 * SIZE : 3 * SIZE, :] = jnp.zeros((SIZE, LANES), F32)
            for j in range(2):
                spread[j, p, k, 0:SIZE, :] = jnp.zeros((SIZE, LANES), F32)
                spread[j, p, k, 2 * SIZE : 3 * SIZE, :] = jnp.zeros((SIZE, LANES), F32)
    acc[...] = jnp.zeros_like(acc)
    term[...] = jnp.zeros_like(term)

    @pl.loop(1, n_pos)
    def _(s):
        meta_copy(s).wait()

    to_scalars = pltpu.make_async_copy(meta_in, meta, meta_sem)
    to_scalars.start()
    to_scalars.wait()
    for c in loads[2:]:
        c.wait()

    @pl.loop(0, n_pos)
    def _(s):
        @pl.loop(chosen(s, (AT_ONCE,) + STARTED[:-1]) + 1, chosen(s, STARTED) + 1)
        def _(m):
            send(m)

        @pl.when(s > 0)
        def _():
            amp_copy(s).wait_recv()

        row = [meta[s, 0, 2 * j] for j in range(2)]
        col = [meta[s, 0, 2 * j + 1] for j in range(2)]
        amp = landed.at[s]
        for j in range(2):
            extract(row[j], col[j], tile, probe, window, psi, j)
        turn(jnp.dot(left[...], psi[...], preferred_element_type=F32), half)
        wave[...] = jnp.dot(half[...], right[...], preferred_element_type=F32)
        for j in range(2):
            modulus(wave, amp, diff, j)
        turn(jnp.dot(right[...], diff[...], preferred_element_type=F32), half)
        chi[...] = jnp.dot(half[...], left[...], preferred_element_type=F32)
        for j in range(2):
            gradients(col[j], chi, probe, window, spread, term, j)
        accumulate(row, spread, acc)

    across = SIZE // LANES
    for plane in range(2):
        for i in range(SIZE // 16):
            for k in range(across):
                values = term[plane, 16 * i : 16 * i + 16, k * LANES : (k + 1) * LANES]
                exact[(plane * (SIZE // 16) + i) * across + k] = values
                rounded[(plane * (SIZE // 16) + i) * across + k] = values.astype(BF16)

    first = SIZE // 16 * across
    a_size, b_size = first // n_obj, first // n_pos
    of_a = lambda o: pl.ds(o * a_size, a_size)
    of_b = lambda p: pl.ds(first + p * b_size, b_size)

    def phase(base, a_of, b_of):
        copies = []
        for d, o in enumerate(peer_o):
            copies.append(((me_p, o), *a_of(d, o)))
        for d, p in enumerate(peer_p):
            copies.append(((p, me_o), *b_of(d, p)))
        copies = [
            pltpu.make_async_remote_copy(
                src_ref=source, dst_ref=target,
                send_sem=sum_send.at[base + i], recv_sem=sum_recv.at[base + i],
                device_id=device, device_id_type=MESH,
            )
            for i, (device, source, target) in enumerate(copies)
        ]
        for c in copies:
            c.start()
        return copies

    step = n_obj - 1 + n_pos - 1
    one = phase(
        0,
        lambda d, o: (rounded.at[of_a(o)], got_a.at[d]),
        lambda d, p: (rounded.at[of_b(p)], got_b.at[d]),
    )
    for c in halos:
        c.wait()
    middle = jnp.zeros((LANES - 16, tall), F32)
    for p in range(2):
        sides[p] = jnp.concatenate([edge_in[1, p], middle, edge_in[0, p]], axis=0).T
    lanes = lax.broadcasted_iota(jnp.int32, (STRIP, LANES), 1)
    for p in range(2):
        for s in range(0, tall, STRIP):
            here = [ext[p, 8 + s : 8 + s + STRIP, k * LANES : (k + 1) * LANES] for k in range(3)]
            here.append(sides[p, s : s + STRIP, :])
            right_of = [pltpu.roll(t, LANES - 1, 1) for t in here]
            left_of = [pltpu.roll(t, 1, 1) for t in here]
            for k in range(3):
                block = slice(k * LANES, (k + 1) * LANES)
                around = ext[p, 7 + s : 7 + s + STRIP, block] + ext[p, 9 + s : 9 + s + STRIP, block]
                around += jnp.where(lanes == 0, left_of[k - 1], left_of[k])
                around += jnp.where(lanes == LANES - 1, right_of[k + 1], right_of[k])
                object_out[p, s : s + STRIP, block] = (
                    0.5 * here[k] + 0.125 * around - 0.25 * acc[p, k, s : s + STRIP, :]
                )

    pltpu.make_async_copy(object_out, object_hbm, out_sem).start()

    @pl.loop(1, n_pos)
    def _(s):
        amp_copy(s).wait_send()

    for c in one:
        c.wait_recv()
    total = exact[of_a(me_o)]
    for d in range(n_obj - 1):
        total += got_a[d].astype(F32)
    all_a[me_p] = total.astype(BF16)
    total = exact[of_b(me_p)]
    for d in range(n_pos - 1):
        total += got_b[d].astype(F32)
    all_b[me_o] = total.astype(BF16)
    two = phase(
        step,
        lambda d, o: (all_b.at[me_o], all_b.at[me_o]),
        lambda d, p: (all_a.at[me_p], all_a.at[me_p]),
    )
    for c in two:
        c.wait_recv()
    total = all_a[0].astype(F32)
    for d in range(1, n_pos):
        total += all_a[d].astype(F32)
    done[of_a(me_o)] = total
    total = all_b[0].astype(F32)
    for d in range(1, n_obj):
        total += all_b[d].astype(F32)
    done[of_b(me_p)] = total
    three = phase(
        2 * step,
        lambda d, o: (done.at[of_a(me_o)], done.at[of_a(me_o)]),
        lambda d, p: (done.at[of_b(me_p)], done.at[of_b(me_p)]),
    )
    for c in three:
        c.wait_recv()
    for plane in range(2):
        for i in range(SIZE // 16):
            for k in range(across):
                here, block = slice(16 * i, 16 * i + 16), slice(k * LANES, (k + 1) * LANES)
                probe_out[plane, here, block] = probe[plane, here, block] - scale * done[
                    (plane * (SIZE // 16) + i) * across + k
                ]
    for c in one + two + three:
        c.wait_send()
    pltpu.make_async_copy(object_out, object_hbm, out_sem).wait()


def fused(owner, rows, cols, amps, obj, probe, left, right, n_pos, n_obj, scale):
    smem = pl.BlockSpec(memory_space=pltpu.SMEM)
    vmem = pl.BlockSpec(memory_space=pltpu.VMEM)
    hbm = pl.BlockSpec(memory_space=pl.ANY)
    count = 3 * (n_pos + n_obj - 2)
    pieces = 2 * SIZE * SIZE // (16 * LANES)
    a_size, b_size = pieces // 2 // n_obj, pieces // 2 // n_pos
    double = (2 * SIZE, 2 * SIZE)
    dma = pltpu.SemaphoreType.DMA
    return pl.pallas_call(
        functools.partial(fused_kernel, n_pos, n_obj, scale),
        out_shape=(
            jax.ShapeDtypeStruct(obj.shape, F32),
            jax.ShapeDtypeStruct(probe.shape, F32),
        ),
        in_specs=[smem, smem, smem, hbm, hbm, hbm, hbm, hbm],
        out_specs=(hbm, vmem),
        scratch_shapes=[
            pltpu.VMEM(amps.shape, BF16),
            pltpu.VMEM(probe.shape, F32),
            pltpu.VMEM(double, BF16),
            pltpu.VMEM(double, BF16),
            pltpu.VMEM(obj.shape, F32),
            pltpu.VMEM((n_pos, CAPACITY, SIZE, SIZE), BF16),
            pltpu.VMEM((n_pos, CAPACITY, SIZE, SIZE), BF16),
            pltpu.VMEM((n_pos, 8, LANES), jnp.int32),
            pltpu.VMEM((n_pos, 8, LANES), jnp.int32),
            pltpu.SMEM((n_pos, 8, LANES), jnp.int32),
            pltpu.VMEM((2, 3, 3 * SIZE, LANES), F32),
            pltpu.VMEM((2, 2, SIZE, SIZE), F32),
            pltpu.VMEM(double, BF16),
            pltpu.VMEM(double, BF16),
            pltpu.VMEM(double, F32),
            pltpu.VMEM(double, BF16),
            pltpu.VMEM(double, F32),
            pltpu.VMEM((2, 2, 3, 3 * SIZE, LANES), F32),
            pltpu.VMEM((2, 3, 2 * SIZE, LANES), F32),
            pltpu.VMEM((2, SIZE, SIZE), F32),
            pltpu.VMEM((pieces, 16, LANES), F32),
            pltpu.VMEM((pieces, 16, LANES), BF16),
            pltpu.VMEM((n_obj - 1, a_size, 16, LANES), BF16),
            pltpu.VMEM((n_pos - 1, b_size, 16, LANES), BF16),
            pltpu.VMEM((n_pos, a_size, 16, LANES), BF16),
            pltpu.VMEM((n_obj, b_size, 16, LANES), BF16),
            pltpu.VMEM((pieces, 16, LANES), F32),
            pltpu.SMEM((n_pos, CAPACITY), jnp.int32),
            pltpu.VMEM((2, 2 * SIZE + 16, 3 * LANES), F32),
            pltpu.VMEM((2, 2, 8, 2 * SIZE), F32),
            pltpu.VMEM((2, 2, 8, 2 * SIZE), F32),
            pltpu.VMEM((2, 2 * SIZE, LANES), F32),
            dma((5,)), dma((n_pos,)), dma((n_pos,)), dma((n_pos,)), dma((n_pos,)), dma,
            dma((count,)), dma((count,)), dma((4,)), dma((4,)), dma,
        ],
        compiler_params=pltpu.CompilerParams(
            collective_id=1, has_side_effects=True, vmem_limit_bytes=56 << 20
        ),
        cost_estimate=pl.CostEstimate(
            flops=2 * n_pos * 32 * SIZE**3, bytes_accessed=16 << 20, transcendentals=0
        ),
        name="fused",
    )(owner, rows, cols, amps, obj, probe, left, right)


def shards(object_field, probe, amplitude, row_offset, col_offset, owner):
    n_pos = lax.axis_size("pos")
    n_obj = lax.axis_size("obj")
    pos_dev = amplitude.shape[0]
    left, right = dft_blocks()
    scale = 1.0 / math.sqrt(pos_dev * n_pos * n_obj)
    return fused(
        owner, row_offset, col_offset, amplitude, object_field, probe, left, right,
        n_pos, n_obj, scale,
    )


def solution(mesh):
    placed = (
        P(None, "obj", "pos"),
        P(),
        P(("pos", "obj"), None, None),
        P(("pos", "obj")),
        P(("pos", "obj")),
        P(("pos", "obj")),
    )
    return jax.shard_map(
        shards, mesh=mesh, in_specs=placed, out_specs=(P(None, "obj", "pos"), P()), check_vma=False
    )
```

```python
import functools
import math

import jax
import jax.numpy as jnp
import numpy as np
from jax import lax
from jax.experimental import pallas as pl
from jax.experimental.pallas import tpu as pltpu
from jax.sharding import PartitionSpec as P

SIZE = 256
CAPACITY = 2
LANES = 128
F32 = jnp.float32
BF16 = jnp.bfloat16


def dft_blocks():
    index = np.arange(SIZE, dtype=np.int64)
    product = (index[:, None] * index[None, :]) % SIZE
    angle = product.astype(np.float32) * np.float32(2.0 * math.pi / SIZE)
    scale = 1.0 / math.sqrt(SIZE)
    real = (np.cos(angle.astype(np.float64)) * scale).astype(np.float32)
    imag = (-np.sin(angle.astype(np.float64)) * scale).astype(np.float32)
    real = jnp.asarray(real).astype(BF16)
    imag = jnp.asarray(imag).astype(BF16)
    top = jnp.concatenate([real, -imag], axis=1)
    bottom = jnp.concatenate([imag, real], axis=1)
    left = jnp.concatenate([top, bottom], axis=0)
    top = jnp.concatenate([real, imag], axis=1)
    bottom = jnp.concatenate([-imag, real], axis=1)
    return left, jnp.concatenate([top, bottom], axis=0)


STRIP = 32


def extract(meta_row, meta_col, tile, probe, window, psi, j):
    lane = lax.broadcasted_iota(jnp.int32, (STRIP, LANES), 1)
    first = lane < LANES - meta_col
    shift = lax.rem(LANES - meta_col, LANES)
    for s in range(0, SIZE, STRIP):
        parts = []
        for p in range(2):
            t = [
                pltpu.roll(tile[p, k, pl.ds(meta_row + s, STRIP), :], shift, 1)
                for k in range(3)
            ]
            parts.append([jnp.where(first, t[k], t[k + 1]) for k in range(2)])
        for k in range(2):
            cols = slice(k * LANES, (k + 1) * LANES)
            x_re, x_im = parts[0][k], parts[1][k]
            window[j, 0, s : s + STRIP, cols] = x_re
            window[j, 1, s : s + STRIP, cols] = x_im
            p_re = probe[0, s : s + STRIP, cols]
            p_im = probe[1, s : s + STRIP, cols]
            out = slice(j * SIZE + k * LANES, j * SIZE + (k + 1) * LANES)
            psi[s : s + STRIP, out] = (p_re * x_re - p_im * x_im).astype(BF16)
            psi[SIZE + s : SIZE + s + STRIP, out] = (p_re * x_im + p_im * x_re).astype(BF16)


def turn(value, out):
    for j in range(2):
        for part in range(2):
            out[j * SIZE : (j + 1) * SIZE, part * SIZE : (part + 1) * SIZE] = value[
                part * SIZE : (part + 1) * SIZE, j * SIZE : (j + 1) * SIZE
            ].astype(BF16)


def modulus(wave, amp, diff, j):
    for s in range(0, SIZE, STRIP):
        rows = slice(j * SIZE + s, j * SIZE + s + STRIP)
        w_re = wave[rows, 0:SIZE]
        w_im = wave[rows, SIZE : 2 * SIZE]
        a = amp[j, s : s + STRIP, :].astype(F32)
        power = w_re * w_re + w_im * w_im
        factor = 1.0 - a * lax.rsqrt(jnp.maximum(power, 0.25))
        cols = slice(j * SIZE, (j + 1) * SIZE)
        diff[s : s + STRIP, cols] = (w_re * factor).astype(BF16)
        diff[SIZE + s : SIZE + s + STRIP, cols] = (w_im * factor).astype(BF16)


def gradients(meta_col, chi, probe, window, spread, term, j):
    lane = lax.broadcasted_iota(jnp.int32, (STRIP, LANES), 1)
    later = lane >= meta_col
    shift = lax.rem(meta_col, LANES)
    zero = jnp.zeros((STRIP, LANES), F32)
    for s in range(0, SIZE, STRIP):
        rows = slice(j * SIZE + s, j * SIZE + s + STRIP)
        turned = [[], []]
        for k in range(2):
            cols = slice(k * LANES, (k + 1) * LANES)
            c_re = chi[rows, k * LANES : (k + 1) * LANES]
            c_im = chi[rows, SIZE + k * LANES : SIZE + (k + 1) * LANES]
            x_re = window[j, 0, s : s + STRIP, cols]
            x_im = window[j, 1, s : s + STRIP, cols]
            term[0, s : s + STRIP, cols] += x_re * c_re + x_im * c_im
            term[1, s : s + STRIP, cols] += x_re * c_im - x_im * c_re
            p_re = probe[0, s : s + STRIP, cols]
            p_im = probe[1, s : s + STRIP, cols]
            g_re = (p_re * c_re + p_im * c_im).astype(BF16).astype(F32)
            g_im = (p_re * c_im - p_im * c_re).astype(BF16).astype(F32)
            turned[0].append(pltpu.roll(g_re, shift, 1))
            turned[1].append(pltpu.roll(g_im, shift, 1))
        here = slice(SIZE + s, SIZE + s + STRIP)
        for p in range(2):
            low, high = turned[p]
            spread[j, p, 0, here, :] = jnp.where(later, low, zero)
            spread[j, p, 1, here, :] = jnp.where(later, high, low)
            spread[j, p, 2, here, :] = jnp.where(later, zero, high)


def accumulate(meta_row, spread, acc):
    starts = [SIZE - jnp.bitwise_and(meta_row[j], 2 * SIZE - 1) for j in range(2)]
    for p in range(2):
        for k in range(3):
            for s in range(0, 2 * SIZE, STRIP):
                acc[p, k, s : s + STRIP, :] += (
                    spread[0, p, k, pl.ds(starts[0] + s, STRIP), :]
                    + spread[1, p, k, pl.ds(starts[1] + s, STRIP), :]
                )


MESH = pl.DeviceIdType.MESH


ORDER = (
    (0, 0),
    (0, 1), (0, 3), (1, 0), (3, 0),
    (1, 1), (3, 3), (1, 3), (3, 1),
    (1, 2), (3, 2), (2, 0),
    (2, 1), (2, 3), (0, 2),
    (2, 2),
)
AT_ONCE = 4
STARTED = (6, 6, 8, 8, 11, 11, 11, 14, 14, 14, 15, 15, 15, 15, 15, 15)


def chosen(s, table):
    return sum(jnp.where(s == i, v, 0) for i, v in enumerate(table) if v)


def fused_kernel(
    n_pos, n_obj, scale,
    owner, rows, cols, amps_hbm, obj_hbm, probe_hbm, left_hbm, right_hbm,
    object_out, probe_out,
    amps, probe, left, right,
    slots, landed, meta_out, meta_in, meta, tile, window, psi, half, wave, diff, chi, spread, acc,
    term, exact, rounded, got_a, got_b, all_a, all_b, done, picked, ext, edge_out, edge_in, sides,
    load_sem, amp_send, amp_recv, meta_send, meta_recv, meta_sem, sum_send, sum_recv,
    halo_send, halo_recv,
):
    tall = 2 * SIZE
    inner = ext.at[:, pl.ds(8, tall), :]
    loads = [
        pltpu.make_async_copy(source, target, load_sem.at[i])
        for i, (source, target) in enumerate(
            ((amps_hbm, amps), (obj_hbm, inner), (probe_hbm, probe), (left_hbm, left), (right_hbm, right))
        )
    ]
    for c in loads:
        c.start()
    me_p = lax.axis_index("pos")
    me_o = lax.axis_index("obj")
    side = math.isqrt(n_pos)
    peer_o = [lax.rem(me_o + d, n_obj) for d in range(1, n_obj)]


    def peer_at(s):
        if isinstance(s, int):
            dx, dy = ORDER[s]
        else:
            dx = chosen(s, [d[0] for d in ORDER])
            dy = chosen(s, [d[1] for d in ORDER])
        x = lax.rem(me_p // side + dx, side)
        y = lax.rem(me_p % side + dy, side)
        return x * side + y

    peer_p = [peer_at(s) for s in range(1, n_pos)]

    barrier = pltpu.get_barrier_semaphore()
    for o in peer_o:
        pl.semaphore_signal(barrier, inc=1, device_id=(me_p, o), device_id_type=MESH)
    for p in peer_p:
        pl.semaphore_signal(barrier, inc=1, device_id=(p, me_o), device_id_type=MESH)
    pl.semaphore_wait(barrier, n_obj + n_pos - 2)

    def amp_copy(s):
        return pltpu.make_async_remote_copy(
            src_ref=slots.at[s], dst_ref=landed.at[s],
            send_sem=amp_send.at[s], recv_sem=amp_recv.at[s],
            device_id=(peer_at(s), me_o), device_id_type=MESH,
        )

    def meta_copy(s):
        return pltpu.make_async_remote_copy(
            src_ref=meta_out.at[s], dst_ref=meta_in.at[s],
            send_sem=meta_send.at[s], recv_sem=meta_recv.at[s],
            device_id=(peer_at(s), me_o), device_id_type=MESH,
        )

    lane = lax.broadcasted_iota(jnp.int32, (8, LANES), 1)

    def announce(s, corners):
        target = peer_at(s)
        first = jnp.int32(-1)
        second = jnp.int32(-1)
        for i in reversed(range(amps.shape[0])):
            hit = owner[i] == target
            second = jnp.where(hit, first, second)
            first = jnp.where(hit, i, first)
        values = jnp.zeros((8, LANES), jnp.int32)
        for k, found in enumerate((first, second)):
            i = jnp.maximum(found, 0)
            picked[s, k] = i
            row = jnp.where(found < 0, 2 * SIZE, rows[i])
            values = jnp.where(lane == 2 * k, row, values)
            values = jnp.where(lane == 2 * k + 1, cols[i], values)
        corners[s] = values

    def lay_out(s, out):
        for k in range(CAPACITY):
            out[s, k] = amps[picked[s, k]]

    def send(s):
        lay_out(s, slots)
        amp_copy(s).start()

    loads[0].wait()

    @pl.loop(1, 1 + AT_ONCE)
    def _(s):
        announce(s, meta_out)
        meta_copy(s).start()
        send(s)

    @pl.loop(1 + AT_ONCE, n_pos)
    def _(s):
        announce(s, meta_out)
        meta_copy(s).start()

    announce(0, meta_in)
    lay_out(0, landed)
    loads[1].wait()

    next_p, last_p = lax.rem(me_p + 1, n_pos), lax.rem(me_p + n_pos - 1, n_pos)
    next_o, last_o = lax.rem(me_o + 1, n_obj), lax.rem(me_o + n_obj - 1, n_obj)

    def halo(i, source, target, device):
        return pltpu.make_async_remote_copy(
            src_ref=source, dst_ref=target, send_sem=halo_send.at[i], recv_sem=halo_recv.at[i],
            device_id=device, device_id_type=MESH,
        )

    for p in range(2):
        edge_out[0, p] = ext[p, 8 : tall + 8, 2 * LANES : 3 * LANES].T[LANES - 8 : LANES]
        edge_out[1, p] = ext[p, 8 : tall + 8, 0:LANES].T[0:8]
    halos = [
        halo(0, ext.at[:, pl.ds(tall, 8), :], ext.at[:, pl.ds(0, 8), :], (me_p, next_o)),
        halo(1, ext.at[:, pl.ds(8, 8), :], ext.at[:, pl.ds(tall + 8, 8), :], (me_p, last_o)),
        halo(2, edge_out.at[0], edge_in.at[0], (next_p, me_o)),
        halo(3, edge_out.at[1], edge_in.at[1], (last_p, me_o)),
    ]
    for c in halos:
        c.start()
    for p in range(2):
        for k in range(3):
            block = slice(k * LANES, (k + 1) * LANES)
            tile[p, k, 0 : 2 * SIZE, :] = ext[p, 8 : tall + 8, block].astype(BF16).astype(F32)
            tile[p, k, 2 * SIZE : 3 * SIZE, :] = jnp.zeros((SIZE, LANES), F32)
            for j in range(2):
                spread[j, p, k, 0:SIZE, :] = jnp.zeros((SIZE, LANES), F32)
                spread[j, p, k, 2 * SIZE : 3 * SIZE, :] = jnp.zeros((SIZE, LANES), F32)
    acc[...] = jnp.zeros_like(acc)
    term[...] = jnp.zeros_like(term)

    @pl.loop(1, n_pos)
    def _(s):
        meta_copy(s).wait()

    to_scalars = pltpu.make_async_copy(meta_in, meta, meta_sem)
    to_scalars.start()
    to_scalars.wait()
    for c in loads[2:]:
        c.wait()

    @pl.loop(0, n_pos)
    def _(s):
        @pl.loop(chosen(s, (AT_ONCE,) + STARTED[:-1]) + 1, chosen(s, STARTED) + 1)
        def _(m):
            send(m)

        @pl.when(s > 0)
        def _():
            amp_copy(s).wait_recv()

        row = [meta[s, 0, 2 * j] for j in range(2)]
        col = [meta[s, 0, 2 * j + 1] for j in range(2)]
        amp = landed.at[s]
        for j in range(2):
            extract(row[j], col[j], tile, probe, window, psi, j)
        turn(jnp.dot(left[...], psi[...], preferred_element_type=F32), half)
        wave[...] = jnp.dot(half[...], right[...], preferred_element_type=F32)
        for j in range(2):
            modulus(wave, amp, diff, j)
        turn(jnp.dot(right[...], diff[...], preferred_element_type=F32), half)
        chi[...] = jnp.dot(half[...], left[...], preferred_element_type=F32)
        for j in range(2):
            gradients(col[j], chi, probe, window, spread, term, j)
        accumulate(row, spread, acc)

    across = SIZE // LANES
    for plane in range(2):
        for i in range(SIZE // 16):
            for k in range(across):
                values = term[plane, 16 * i : 16 * i + 16, k * LANES : (k + 1) * LANES]
                exact[(plane * (SIZE // 16) + i) * across + k] = values
                rounded[(plane * (SIZE // 16) + i) * across + k] = values.astype(BF16)

    first = SIZE // 16 * across
    a_size, b_size = first // n_obj, first // n_pos
    of_a = lambda o: pl.ds(o * a_size, a_size)
    of_b = lambda p: pl.ds(first + p * b_size, b_size)

    def phase(base, a_of, b_of):
        copies = []
        for d, o in enumerate(peer_o):
            copies.append(((me_p, o), *a_of(d, o)))
        for d, p in enumerate(peer_p):
            copies.append(((p, me_o), *b_of(d, p)))
        copies = [
            pltpu.make_async_remote_copy(
                src_ref=source, dst_ref=target,
                send_sem=sum_send.at[base + i], recv_sem=sum_recv.at[base + i],
                device_id=device, device_id_type=MESH,
            )
            for i, (device, source, target) in enumerate(copies)
        ]
        for c in copies:
            c.start()
        return copies

    step = n_obj - 1 + n_pos - 1
    one = phase(
        0,
        lambda d, o: (rounded.at[of_a(o)], got_a.at[d]),
        lambda d, p: (rounded.at[of_b(p)], got_b.at[d]),
    )
    for c in halos:
        c.wait()
    middle = jnp.zeros((LANES - 16, tall), F32)
    for p in range(2):
        sides[p] = jnp.concatenate([edge_in[1, p], middle, edge_in[0, p]], axis=0).T
    lanes = lax.broadcasted_iota(jnp.int32, (STRIP, LANES), 1)
    for p in range(2):
        for s in range(0, tall, STRIP):
            here = [ext[p, 8 + s : 8 + s + STRIP, k * LANES : (k + 1) * LANES] for k in range(3)]
            here.append(sides[p, s : s + STRIP, :])
            right_of = [pltpu.roll(t, LANES - 1, 1) for t in here]
            left_of = [pltpu.roll(t, 1, 1) for t in here]
            for k in range(3):
                block = slice(k * LANES, (k + 1) * LANES)
                around = ext[p, 7 + s : 7 + s + STRIP, block] + ext[p, 9 + s : 9 + s + STRIP, block]
                around += jnp.where(lanes == 0, left_of[k - 1], left_of[k])
                around += jnp.where(lanes == LANES - 1, right_of[k + 1], right_of[k])
                object_out[p, s : s + STRIP, block] = (
                    0.5 * here[k] + 0.125 * around - 0.25 * acc[p, k, s : s + STRIP, :]
                )


    @pl.loop(1, n_pos)
    def _(s):
        amp_copy(s).wait_send()

    for c in one:
        c.wait_recv()
    total = exact[of_a(me_o)]
    for d in range(n_obj - 1):
        total += got_a[d].astype(F32)
    all_a[me_p] = total.astype(BF16)
    total = exact[of_b(me_p)]
    for d in range(n_pos - 1):
        total += got_b[d].astype(F32)
    all_b[me_o] = total.astype(BF16)
    two = phase(
        step,
        lambda d, o: (all_b.at[me_o], all_b.at[me_o]),
        lambda d, p: (all_a.at[me_p], all_a.at[me_p]),
    )
    for c in two:
        c.wait_recv()
    total = all_a[0].astype(F32)
    for d in range(1, n_pos):
        total += all_a[d].astype(F32)
    done[of_a(me_o)] = total
    total = all_b[0].astype(F32)
    for d in range(1, n_obj):
        total += all_b[d].astype(F32)
    done[of_b(me_p)] = total
    three = phase(
        2 * step,
        lambda d, o: (done.at[of_a(me_o)], done.at[of_a(me_o)]),
        lambda d, p: (done.at[of_b(me_p)], done.at[of_b(me_p)]),
    )
    for c in three:
        c.wait_recv()
    for plane in range(2):
        for i in range(SIZE // 16):
            for k in range(across):
                here, block = slice(16 * i, 16 * i + 16), slice(k * LANES, (k + 1) * LANES)
                probe_out[plane, here, block] = probe[plane, here, block] - scale * done[
                    (plane * (SIZE // 16) + i) * across + k
                ]
    for c in one + two + three:
        c.wait_send()


def fused(owner, rows, cols, amps, obj, probe, left, right, n_pos, n_obj, scale):
    smem = pl.BlockSpec(memory_space=pltpu.SMEM)
    vmem = pl.BlockSpec(memory_space=pltpu.VMEM)
    hbm = pl.BlockSpec(memory_space=pl.ANY)
    count = 3 * (n_pos + n_obj - 2)
    pieces = 2 * SIZE * SIZE // (16 * LANES)
    a_size, b_size = pieces // 2 // n_obj, pieces // 2 // n_pos
    double = (2 * SIZE, 2 * SIZE)
    dma = pltpu.SemaphoreType.DMA
    return pl.pallas_call(
        functools.partial(fused_kernel, n_pos, n_obj, scale),
        out_shape=(
            pltpu.VMEM(obj.shape, F32),
            pltpu.VMEM(probe.shape, F32),
        ),
        in_specs=[smem, smem, smem, hbm, hbm, hbm, hbm, hbm],
        out_specs=(vmem, vmem),
        scratch_shapes=[
            pltpu.VMEM(amps.shape, BF16),
            pltpu.VMEM(probe.shape, F32),
            pltpu.VMEM(double, BF16),
            pltpu.VMEM(double, BF16),
            pltpu.VMEM((n_pos, CAPACITY, SIZE, SIZE), BF16),
            pltpu.VMEM((n_pos, CAPACITY, SIZE, SIZE), BF16),
            pltpu.VMEM((n_pos, 8, LANES), jnp.int32),
            pltpu.VMEM((n_pos, 8, LANES), jnp.int32),
            pltpu.SMEM((n_pos, 8, LANES), jnp.int32),
            pltpu.VMEM((2, 3, 3 * SIZE, LANES), F32),
            pltpu.VMEM((2, 2, SIZE, SIZE), F32),
            pltpu.VMEM(double, BF16),
            pltpu.VMEM(double, BF16),
            pltpu.VMEM(double, F32),
            pltpu.VMEM(double, BF16),
            pltpu.VMEM(double, F32),
            pltpu.VMEM((2, 2, 3, 3 * SIZE, LANES), F32),
            pltpu.VMEM((2, 3, 2 * SIZE, LANES), F32),
            pltpu.VMEM((2, SIZE, SIZE), F32),
            pltpu.VMEM((pieces, 16, LANES), F32),
            pltpu.VMEM((pieces, 16, LANES), BF16),
            pltpu.VMEM((n_obj - 1, a_size, 16, LANES), BF16),
            pltpu.VMEM((n_pos - 1, b_size, 16, LANES), BF16),
            pltpu.VMEM((n_pos, a_size, 16, LANES), BF16),
            pltpu.VMEM((n_obj, b_size, 16, LANES), BF16),
            pltpu.VMEM((pieces, 16, LANES), F32),
            pltpu.SMEM((n_pos, CAPACITY), jnp.int32),
            pltpu.VMEM((2, 2 * SIZE + 16, 3 * LANES), F32),
            pltpu.VMEM((2, 2, 8, 2 * SIZE), F32),
            pltpu.VMEM((2, 2, 8, 2 * SIZE), F32),
            pltpu.VMEM((2, 2 * SIZE, LANES), F32),
            dma((5,)), dma((n_pos,)), dma((n_pos,)), dma((n_pos,)), dma((n_pos,)), dma,
            dma((count,)), dma((count,)), dma((4,)), dma((4,)),
        ],
        compiler_params=pltpu.CompilerParams(
            collective_id=1, has_side_effects=True, vmem_limit_bytes=52 << 20
        ),
        cost_estimate=pl.CostEstimate(
            flops=2 * n_pos * 32 * SIZE**3, bytes_accessed=16 << 20, transcendentals=0
        ),
        name="fused",
    )(owner, rows, cols, amps, obj, probe, left, right)


def shards(object_field, probe, amplitude, row_offset, col_offset, owner):
    n_pos = lax.axis_size("pos")
    n_obj = lax.axis_size("obj")
    pos_dev = amplitude.shape[0]
    left, right = dft_blocks()
    scale = 1.0 / math.sqrt(pos_dev * n_pos * n_obj)
    return fused(
        owner, row_offset, col_offset, amplitude, object_field, probe, left, right,
        n_pos, n_obj, scale,
    )


def solution(mesh):
    placed = (
        P(None, "obj", "pos"),
        P(),
        P(("pos", "obj"), None, None),
        P(("pos", "obj")),
        P(("pos", "obj")),
        P(("pos", "obj")),
    )
    return jax.shard_map(
        shards, mesh=mesh, in_specs=placed, out_specs=(P(None, "obj", "pos"), P()), check_vma=False
    )
```

```python
import functools
import math

import jax
import jax.numpy as jnp
import numpy as np
from jax import lax
from jax.experimental import pallas as pl
from jax.experimental.pallas import tpu as pltpu
from jax.sharding import PartitionSpec as P

SIZE = 256
CAPACITY = 2
LANES = 128
F32 = jnp.float32
BF16 = jnp.bfloat16


def dft_blocks():
    index = np.arange(SIZE, dtype=np.int64)
    product = (index[:, None] * index[None, :]) % SIZE
    angle = product.astype(np.float32) * np.float32(2.0 * math.pi / SIZE)
    scale = 1.0 / math.sqrt(SIZE)
    real = (np.cos(angle.astype(np.float64)) * scale).astype(np.float32)
    imag = (-np.sin(angle.astype(np.float64)) * scale).astype(np.float32)
    real = jnp.asarray(real).astype(BF16)
    imag = jnp.asarray(imag).astype(BF16)
    top = jnp.concatenate([real, -imag], axis=1)
    bottom = jnp.concatenate([imag, real], axis=1)
    left = jnp.concatenate([top, bottom], axis=0)
    top = jnp.concatenate([real, imag], axis=1)
    bottom = jnp.concatenate([-imag, real], axis=1)
    return left, jnp.concatenate([top, bottom], axis=0)


STRIP = 32


def extract(meta_row, meta_col, tile, probe, window, psi, j):
    lane = lax.broadcasted_iota(jnp.int32, (STRIP, LANES), 1)
    first = lane < LANES - meta_col
    shift = lax.rem(LANES - meta_col, LANES)
    for s in range(0, SIZE, STRIP):
        parts = []
        for p in range(2):
            t = [
                pltpu.roll(tile[p, k, pl.ds(meta_row + s, STRIP), :], shift, 1)
                for k in range(3)
            ]
            parts.append([jnp.where(first, t[k], t[k + 1]) for k in range(2)])
        for k in range(2):
            cols = slice(k * LANES, (k + 1) * LANES)
            x_re, x_im = parts[0][k], parts[1][k]
            window[j, 0, s : s + STRIP, cols] = x_re
            window[j, 1, s : s + STRIP, cols] = x_im
            p_re = probe[0, s : s + STRIP, cols]
            p_im = probe[1, s : s + STRIP, cols]
            out = slice(j * SIZE + k * LANES, j * SIZE + (k + 1) * LANES)
            psi[s : s + STRIP, out] = (p_re * x_re - p_im * x_im).astype(BF16)
            psi[SIZE + s : SIZE + s + STRIP, out] = (p_re * x_im + p_im * x_re).astype(BF16)


def turn(value, out):
    for j in range(2):
        for part in range(2):
            out[j * SIZE : (j + 1) * SIZE, part * SIZE : (part + 1) * SIZE] = value[
                part * SIZE : (part + 1) * SIZE, j * SIZE : (j + 1) * SIZE
            ].astype(BF16)


def modulus(wave, amp, diff, j):
    for s in range(0, SIZE, STRIP):
        rows = slice(j * SIZE + s, j * SIZE + s + STRIP)
        w_re = wave[rows, 0:SIZE]
        w_im = wave[rows, SIZE : 2 * SIZE]
        a = amp[j, s : s + STRIP, :].astype(F32)
        power = w_re * w_re + w_im * w_im
        factor = 1.0 - a * lax.rsqrt(jnp.maximum(power, 0.25))
        cols = slice(j * SIZE, (j + 1) * SIZE)
        diff[s : s + STRIP, cols] = (w_re * factor).astype(BF16)
        diff[SIZE + s : SIZE + s + STRIP, cols] = (w_im * factor).astype(BF16)


def gradients(meta_col, chi, probe, window, spread, term, j):
    lane = lax.broadcasted_iota(jnp.int32, (STRIP, LANES), 1)
    later = lane >= meta_col
    shift = lax.rem(meta_col, LANES)
    zero = jnp.zeros((STRIP, LANES), F32)
    for s in range(0, SIZE, STRIP):
        rows = slice(j * SIZE + s, j * SIZE + s + STRIP)
        turned = [[], []]
        for k in range(2):
            cols = slice(k * LANES, (k + 1) * LANES)
            c_re = chi[rows, k * LANES : (k + 1) * LANES]
            c_im = chi[rows, SIZE + k * LANES : SIZE + (k + 1) * LANES]
            x_re = window[j, 0, s : s + STRIP, cols]
            x_im = window[j, 1, s : s + STRIP, cols]
            term[0, s : s + STRIP, cols] += x_re * c_re + x_im * c_im
            term[1, s : s + STRIP, cols] += x_re * c_im - x_im * c_re
            p_re = probe[0, s : s + STRIP, cols]
            p_im = probe[1, s : s + STRIP, cols]
            g_re = (p_re * c_re + p_im * c_im).astype(BF16).astype(F32)
            g_im = (p_re * c_im - p_im * c_re).astype(BF16).astype(F32)
            turned[0].append(pltpu.roll(g_re, shift, 1))
            turned[1].append(pltpu.roll(g_im, shift, 1))
        here = slice(SIZE + s, SIZE + s + STRIP)
        for p in range(2):
            low, high = turned[p]
            spread[j, p, 0, here, :] = jnp.where(later, low, zero)
            spread[j, p, 1, here, :] = jnp.where(later, high, low)
            spread[j, p, 2, here, :] = jnp.where(later, zero, high)


def accumulate(meta_row, spread, acc):
    starts = [SIZE - jnp.bitwise_and(meta_row[j], 2 * SIZE - 1) for j in range(2)]
    for p in range(2):
        for k in range(3):
            for s in range(0, 2 * SIZE, STRIP):
                acc[p, k, s : s + STRIP, :] += (
                    spread[0, p, k, pl.ds(starts[0] + s, STRIP), :]
                    + spread[1, p, k, pl.ds(starts[1] + s, STRIP), :]
                )


MESH = pl.DeviceIdType.MESH


ORDER = (
    (0, 0),
    (0, 1), (0, 3), (1, 0), (3, 0),
    (1, 1), (3, 3), (1, 3), (3, 1),
    (1, 2), (3, 2), (2, 0),
    (2, 1), (2, 3), (0, 2),
    (2, 2),
)
AT_ONCE = 4
STARTED = (6, 6, 8, 8, 11, 11, 11, 14, 15, 15, 15, 15, 15, 15, 15, 15)


def chosen(s, table):
    return sum(jnp.where(s == i, v, 0) for i, v in enumerate(table) if v)


def fused_kernel(
    n_pos, n_obj, scale,
    owner, rows, cols, amps_hbm, obj_hbm, probe_hbm, left_hbm, right_hbm,
    object_out, probe_out,
    amps, probe, left, right,
    slots, landed, meta_out, meta_in, meta, tile, window, psi, half, wave, diff, chi, spread, acc,
    term, exact, rounded, got_a, got_b, all_a, all_b, done, picked, ext, edge_out, edge_in, sides,
    load_sem, amp_send, amp_recv, meta_send, meta_recv, meta_sem, sum_send, sum_recv,
    halo_send, halo_recv,
):
    tall = 2 * SIZE
    inner = ext.at[:, pl.ds(8, tall), :]
    loads = [
        pltpu.make_async_copy(source, target, load_sem.at[i])
        for i, (source, target) in enumerate(
            ((amps_hbm, amps), (obj_hbm, inner), (probe_hbm, probe), (left_hbm, left), (right_hbm, right))
        )
    ]
    for c in loads:
        c.start()
    me_p = lax.axis_index("pos")
    me_o = lax.axis_index("obj")
    side = math.isqrt(n_pos)
    peer_o = [lax.rem(me_o + d, n_obj) for d in range(1, n_obj)]


    def peer_at(s):
        if isinstance(s, int):
            dx, dy = ORDER[s]
        else:
            dx = chosen(s, [d[0] for d in ORDER])
            dy = chosen(s, [d[1] for d in ORDER])
        x = lax.rem(me_p // side + dx, side)
        y = lax.rem(me_p % side + dy, side)
        return x * side + y

    peer_p = [peer_at(s) for s in range(1, n_pos)]

    barrier = pltpu.get_barrier_semaphore()
    for o in peer_o:
        pl.semaphore_signal(barrier, inc=1, device_id=(me_p, o), device_id_type=MESH)
    for p in peer_p:
        pl.semaphore_signal(barrier, inc=1, device_id=(p, me_o), device_id_type=MESH)
    pl.semaphore_wait(barrier, n_obj + n_pos - 2)

    def amp_copy(s):
        return pltpu.make_async_remote_copy(
            src_ref=slots.at[s], dst_ref=landed.at[s],
            send_sem=amp_send.at[s], recv_sem=amp_recv.at[s],
            device_id=(peer_at(s), me_o), device_id_type=MESH,
        )

    def meta_copy(s):
        return pltpu.make_async_remote_copy(
            src_ref=meta_out.at[s], dst_ref=meta_in.at[s],
            send_sem=meta_send.at[s], recv_sem=meta_recv.at[s],
            device_id=(peer_at(s), me_o), device_id_type=MESH,
        )

    lane = lax.broadcasted_iota(jnp.int32, (8, LANES), 1)

    def announce(s, corners):
        target = peer_at(s)
        first = jnp.int32(-1)
        second = jnp.int32(-1)
        for i in reversed(range(amps.shape[0])):
            hit = owner[i] == target
            second = jnp.where(hit, first, second)
            first = jnp.where(hit, i, first)
        values = jnp.zeros((8, LANES), jnp.int32)
        for k, found in enumerate((first, second)):
            i = jnp.maximum(found, 0)
            picked[s, k] = i
            row = jnp.where(found < 0, 2 * SIZE, rows[i])
            values = jnp.where(lane == 2 * k, row, values)
            values = jnp.where(lane == 2 * k + 1, cols[i], values)
        corners[s] = values

    def lay_out(s, out):
        for k in range(CAPACITY):
            out[s, k] = amps[picked[s, k]]

    def send(s):
        lay_out(s, slots)
        amp_copy(s).start()

    loads[0].wait()

    @pl.loop(1, 1 + AT_ONCE)
    def _(s):
        announce(s, meta_out)
        meta_copy(s).start()
        send(s)

    @pl.loop(1 + AT_ONCE, n_pos)
    def _(s):
        announce(s, meta_out)
        meta_copy(s).start()

    announce(0, meta_in)
    lay_out(0, landed)
    loads[1].wait()

    next_p, last_p = lax.rem(me_p + 1, n_pos), lax.rem(me_p + n_pos - 1, n_pos)
    next_o, last_o = lax.rem(me_o + 1, n_obj), lax.rem(me_o + n_obj - 1, n_obj)

    def halo(i, source, target, device):
        return pltpu.make_async_remote_copy(
            src_ref=source, dst_ref=target, send_sem=halo_send.at[i], recv_sem=halo_recv.at[i],
            device_id=device, device_id_type=MESH,
        )

    for p in range(2):
        edge_out[0, p] = ext[p, 8 : tall + 8, 2 * LANES : 3 * LANES].T[LANES - 8 : LANES]
        edge_out[1, p] = ext[p, 8 : tall + 8, 0:LANES].T[0:8]
    halos = [
        halo(0, ext.at[:, pl.ds(tall, 8), :], ext.at[:, pl.ds(0, 8), :], (me_p, next_o)),
        halo(1, ext.at[:, pl.ds(8, 8), :], ext.at[:, pl.ds(tall + 8, 8), :], (me_p, last_o)),
        halo(2, edge_out.at[0], edge_in.at[0], (next_p, me_o)),
        halo(3, edge_out.at[1], edge_in.at[1], (last_p, me_o)),
    ]
    for c in halos:
        c.start()
    for p in range(2):
        for k in range(3):
            block = slice(k * LANES, (k + 1) * LANES)
            tile[p, k, 0 : 2 * SIZE, :] = ext[p, 8 : tall + 8, block].astype(BF16).astype(F32)
            tile[p, k, 2 * SIZE : 3 * SIZE, :] = jnp.zeros((SIZE, LANES), F32)
            for j in range(2):
                spread[j, p, k, 0:SIZE, :] = jnp.zeros((SIZE, LANES), F32)
                spread[j, p, k, 2 * SIZE : 3 * SIZE, :] = jnp.zeros((SIZE, LANES), F32)
    acc[...] = jnp.zeros_like(acc)
    term[...] = jnp.zeros_like(term)

    @pl.loop(1, n_pos)
    def _(s):
        meta_copy(s).wait()

    to_scalars = pltpu.make_async_copy(meta_in, meta, meta_sem)
    to_scalars.start()
    to_scalars.wait()
    for c in loads[2:]:
        c.wait()

    @pl.loop(0, n_pos)
    def _(s):
        @pl.loop(chosen(s, (AT_ONCE,) + STARTED[:-1]) + 1, chosen(s, STARTED) + 1)
        def _(m):
            send(m)

        @pl.when(s > 0)
        def _():
            accumulate([meta[s - 1, 0, 2 * j] for j in range(2)], spread, acc)
            amp_copy(s).wait_recv()

        row = [meta[s, 0, 2 * j] for j in range(2)]
        col = [meta[s, 0, 2 * j + 1] for j in range(2)]
        amp = landed.at[s]
        for j in range(2):
            extract(row[j], col[j], tile, probe, window, psi, j)
        turn(jnp.dot(left[...], psi[...], preferred_element_type=F32), half)
        wave[...] = jnp.dot(half[...], right[...], preferred_element_type=F32)
        for j in range(2):
            modulus(wave, amp, diff, j)
        turn(jnp.dot(right[...], diff[...], preferred_element_type=F32), half)
        chi[...] = jnp.dot(half[...], left[...], preferred_element_type=F32)
        for j in range(2):
            gradients(col[j], chi, probe, window, spread, term, j)

    across = SIZE // LANES
    for plane in range(2):
        for i in range(SIZE // 16):
            for k in range(across):
                values = term[plane, 16 * i : 16 * i + 16, k * LANES : (k + 1) * LANES]
                exact[(plane * (SIZE // 16) + i) * across + k] = values
                rounded[(plane * (SIZE // 16) + i) * across + k] = values.astype(BF16)

    first = SIZE // 16 * across
    a_size, b_size = first // n_obj, first // n_pos
    of_a = lambda o: pl.ds(o * a_size, a_size)
    of_b = lambda p: pl.ds(first + p * b_size, b_size)

    def phase(base, a_of, b_of):
        copies = []
        for d, p in reversed(list(enumerate(peer_p))) if b_of else ():
            copies.append(((p, me_o), *b_of(d, p)))
        for d, o in enumerate(peer_o) if a_of else ():
            copies.append(((me_p, o), *a_of(d, o)))
        copies = [
            pltpu.make_async_remote_copy(
                src_ref=source, dst_ref=target,
                send_sem=sum_send.at[base + i], recv_sem=sum_recv.at[base + i],
                device_id=device, device_id_type=MESH,
            )
            for i, (device, source, target) in enumerate(copies)
        ]
        for c in copies:
            c.start()
        return copies

    step = n_obj - 1 + n_pos - 1
    one = phase(
        0,
        lambda d, o: (rounded.at[of_a(o)], got_a.at[d]),
        lambda d, p: (rounded.at[of_b(p)], got_b.at[d]),
    )
    accumulate([meta[n_pos - 1, 0, 2 * j] for j in range(2)], spread, acc)
    for c in halos:
        c.wait()
    middle = jnp.zeros((LANES - 16, tall), F32)
    for p in range(2):
        sides[p] = jnp.concatenate([edge_in[1, p], middle, edge_in[0, p]], axis=0).T
    lanes = lax.broadcasted_iota(jnp.int32, (STRIP, LANES), 1)
    for p in range(2):
        for s in range(0, tall, STRIP):
            here = [ext[p, 8 + s : 8 + s + STRIP, k * LANES : (k + 1) * LANES] for k in range(3)]
            here.append(sides[p, s : s + STRIP, :])
            right_of = [pltpu.roll(t, LANES - 1, 1) for t in here]
            left_of = [pltpu.roll(t, 1, 1) for t in here]
            for k in range(3):
                block = slice(k * LANES, (k + 1) * LANES)
                around = ext[p, 7 + s : 7 + s + STRIP, block] + ext[p, 9 + s : 9 + s + STRIP, block]
                around += jnp.where(lanes == 0, left_of[k - 1], left_of[k])
                around += jnp.where(lanes == LANES - 1, right_of[k + 1], right_of[k])
                object_out[p, s : s + STRIP, block] = (
                    0.5 * here[k] + 0.125 * around - 0.25 * acc[p, k, s : s + STRIP, :]
                )


    @pl.loop(1, n_pos)
    def _(s):
        amp_copy(s).wait_send()

    for c in one[n_pos - 1 :]:
        c.wait_recv()
    total = exact[of_a(me_o)]
    for d in range(n_obj - 1):
        total += got_a[d].astype(F32)
    all_a[me_p] = total.astype(BF16)
    two = phase(step, None, lambda d, p: (all_a.at[me_p], all_a.at[me_p]))
    for c in one[: n_pos - 1]:
        c.wait_recv()
    total = exact[of_b(me_p)]
    for d in range(n_pos - 1):
        total += got_b[d].astype(F32)
    all_b[me_o] = total.astype(BF16)
    more = phase(step + n_pos - 1, lambda d, o: (all_b.at[me_o], all_b.at[me_o]), None)
    for c in more:
        c.wait_recv()
    total = all_b[0].astype(F32)
    for d in range(1, n_obj):
        total += all_b[d].astype(F32)
    done[of_b(me_p)] = total
    three = phase(2 * step, None, lambda d, p: (done.at[of_b(me_p)], done.at[of_b(me_p)]))
    for c in two:
        c.wait_recv()
    total = all_a[0].astype(F32)
    for d in range(1, n_pos):
        total += all_a[d].astype(F32)
    done[of_a(me_o)] = total
    last = phase(
        2 * step + n_pos - 1, lambda d, o: (done.at[of_a(me_o)], done.at[of_a(me_o)]), None
    )
    for c in three + last:
        c.wait_recv()
    for plane in range(2):
        for i in range(SIZE // 16):
            for k in range(across):
                here, block = slice(16 * i, 16 * i + 16), slice(k * LANES, (k + 1) * LANES)
                probe_out[plane, here, block] = probe[plane, here, block] - scale * done[
                    (plane * (SIZE // 16) + i) * across + k
                ]
    for c in one + two + more + three + last:
        c.wait_send()


def fused(owner, rows, cols, amps, obj, probe, left, right, n_pos, n_obj, scale):
    smem = pl.BlockSpec(memory_space=pltpu.SMEM)
    vmem = pl.BlockSpec(memory_space=pltpu.VMEM)
    hbm = pl.BlockSpec(memory_space=pl.ANY)
    count = 3 * (n_pos + n_obj - 2)
    pieces = 2 * SIZE * SIZE // (16 * LANES)
    a_size, b_size = pieces // 2 // n_obj, pieces // 2 // n_pos
    double = (2 * SIZE, 2 * SIZE)
    dma = pltpu.SemaphoreType.DMA
    return pl.pallas_call(
        functools.partial(fused_kernel, n_pos, n_obj, scale),
        out_shape=(
            pltpu.VMEM(obj.shape, F32),
            pltpu.VMEM(probe.shape, F32),
        ),
        in_specs=[smem, smem, smem, hbm, hbm, hbm, hbm, hbm],
        out_specs=(vmem, vmem),
        scratch_shapes=[
            pltpu.VMEM(amps.shape, BF16),
            pltpu.VMEM(probe.shape, F32),
            pltpu.VMEM(double, BF16),
            pltpu.VMEM(double, BF16),
            pltpu.VMEM((n_pos, CAPACITY, SIZE, SIZE), BF16),
            pltpu.VMEM((n_pos, CAPACITY, SIZE, SIZE), BF16),
            pltpu.VMEM((n_pos, 8, LANES), jnp.int32),
            pltpu.VMEM((n_pos, 8, LANES), jnp.int32),
            pltpu.SMEM((n_pos, 8, LANES), jnp.int32),
            pltpu.VMEM((2, 3, 3 * SIZE, LANES), F32),
            pltpu.VMEM((2, 2, SIZE, SIZE), F32),
            pltpu.VMEM(double, BF16),
            pltpu.VMEM(double, BF16),
            pltpu.VMEM(double, F32),
            pltpu.VMEM(double, BF16),
            pltpu.VMEM(double, F32),
            pltpu.VMEM((2, 2, 3, 3 * SIZE, LANES), F32),
            pltpu.VMEM((2, 3, 2 * SIZE, LANES), F32),
            pltpu.VMEM((2, SIZE, SIZE), F32),
            pltpu.VMEM((pieces, 16, LANES), F32),
            pltpu.VMEM((pieces, 16, LANES), BF16),
            pltpu.VMEM((n_obj - 1, a_size, 16, LANES), BF16),
            pltpu.VMEM((n_pos - 1, b_size, 16, LANES), BF16),
            pltpu.VMEM((n_pos, a_size, 16, LANES), BF16),
            pltpu.VMEM((n_obj, b_size, 16, LANES), BF16),
            pltpu.VMEM((pieces, 16, LANES), F32),
            pltpu.SMEM((n_pos, CAPACITY), jnp.int32),
            pltpu.VMEM((2, 2 * SIZE + 16, 3 * LANES), F32),
            pltpu.VMEM((2, 2, 8, 2 * SIZE), F32),
            pltpu.VMEM((2, 2, 8, 2 * SIZE), F32),
            pltpu.VMEM((2, 2 * SIZE, LANES), F32),
            dma((5,)), dma((n_pos,)), dma((n_pos,)), dma((n_pos,)), dma((n_pos,)), dma,
            dma((count,)), dma((count,)), dma((4,)), dma((4,)),
        ],
        compiler_params=pltpu.CompilerParams(
            collective_id=1, has_side_effects=True, vmem_limit_bytes=52 << 20
        ),
        cost_estimate=pl.CostEstimate(
            flops=2 * n_pos * 32 * SIZE**3, bytes_accessed=16 << 20, transcendentals=0
        ),
        name="fused",
    )(owner, rows, cols, amps, obj, probe, left, right)


def shards(object_field, probe, amplitude, row_offset, col_offset, owner):
    n_pos = lax.axis_size("pos")
    n_obj = lax.axis_size("obj")
    pos_dev = amplitude.shape[0]
    left, right = dft_blocks()
    scale = 1.0 / math.sqrt(pos_dev * n_pos * n_obj)
    return fused(
        owner, row_offset, col_offset, amplitude, object_field, probe, left, right,
        n_pos, n_obj, scale,
    )


def solution(mesh):
    placed = (
        P(None, "obj", "pos"),
        P(),
        P(("pos", "obj"), None, None),
        P(("pos", "obj")),
        P(("pos", "obj")),
        P(("pos", "obj")),
    )
    return jax.shard_map(
        shards, mesh=mesh, in_specs=placed, out_specs=(P(None, "obj", "pos"), P()), check_vma=False
    )
```

```python
import functools
import math

import jax
import jax.numpy as jnp
import numpy as np
from jax import lax
from jax.experimental import pallas as pl
from jax.experimental.pallas import tpu as pltpu
from jax.sharding import PartitionSpec as P

SIZE = 256
CAPACITY = 2
LANES = 128
F32 = jnp.float32
BF16 = jnp.bfloat16


def dft_blocks():
    index = np.arange(SIZE, dtype=np.int64)
    product = (index[:, None] * index[None, :]) % SIZE
    angle = product.astype(np.float32) * np.float32(2.0 * math.pi / SIZE)
    scale = 1.0 / math.sqrt(SIZE)
    real = (np.cos(angle.astype(np.float64)) * scale).astype(np.float32)
    imag = (-np.sin(angle.astype(np.float64)) * scale).astype(np.float32)
    real = jnp.asarray(real).astype(BF16)
    imag = jnp.asarray(imag).astype(BF16)
    top = jnp.concatenate([real, -imag], axis=1)
    bottom = jnp.concatenate([imag, real], axis=1)
    left = jnp.concatenate([top, bottom], axis=0)
    top = jnp.concatenate([real, imag], axis=1)
    bottom = jnp.concatenate([-imag, real], axis=1)
    return left, jnp.concatenate([top, bottom], axis=0)


STRIP = 32


def extract(meta_row, meta_col, tile, probe, window, psi, j):
    lane = lax.broadcasted_iota(jnp.int32, (STRIP, LANES), 1)
    first = lane < LANES - meta_col
    shift = lax.rem(LANES - meta_col, LANES)
    for s in range(0, SIZE, STRIP):
        parts = []
        for p in range(2):
            t = [
                pltpu.roll(tile[p, k, pl.ds(meta_row + s, STRIP), :], shift, 1)
                for k in range(3)
            ]
            parts.append([jnp.where(first, t[k], t[k + 1]) for k in range(2)])
        for k in range(2):
            cols = slice(k * LANES, (k + 1) * LANES)
            x_re, x_im = parts[0][k], parts[1][k]
            window[j, 0, s : s + STRIP, cols] = x_re
            window[j, 1, s : s + STRIP, cols] = x_im
            p_re = probe[0, s : s + STRIP, cols]
            p_im = probe[1, s : s + STRIP, cols]
            out = slice(j * SIZE + k * LANES, j * SIZE + (k + 1) * LANES)
            psi[s : s + STRIP, out] = (p_re * x_re - p_im * x_im).astype(BF16)
            psi[SIZE + s : SIZE + s + STRIP, out] = (p_re * x_im + p_im * x_re).astype(BF16)


def turn(value, out):
    for j in range(2):
        for part in range(2):
            out[j * SIZE : (j + 1) * SIZE, part * SIZE : (part + 1) * SIZE] = value[
                part * SIZE : (part + 1) * SIZE, j * SIZE : (j + 1) * SIZE
            ].astype(BF16)


def modulus(wave, amp, diff, j):
    for s in range(0, SIZE, STRIP):
        rows = slice(j * SIZE + s, j * SIZE + s + STRIP)
        w_re = wave[rows, 0:SIZE]
        w_im = wave[rows, SIZE : 2 * SIZE]
        a = amp[j, s : s + STRIP, :].astype(F32)
        power = w_re * w_re + w_im * w_im
        factor = 1.0 - a * lax.rsqrt(jnp.maximum(power, 0.25))
        cols = slice(j * SIZE, (j + 1) * SIZE)
        diff[s : s + STRIP, cols] = (w_re * factor).astype(BF16)
        diff[SIZE + s : SIZE + s + STRIP, cols] = (w_im * factor).astype(BF16)


def gradients(meta_col, chi, probe, window, spread, term, j):
    lane = lax.broadcasted_iota(jnp.int32, (STRIP, LANES), 1)
    later = lane >= meta_col
    shift = lax.rem(meta_col, LANES)
    zero = jnp.zeros((STRIP, LANES), F32)
    for s in range(0, SIZE, STRIP):
        rows = slice(j * SIZE + s, j * SIZE + s + STRIP)
        turned = [[], []]
        for k in range(2):
            cols = slice(k * LANES, (k + 1) * LANES)
            c_re = chi[rows, k * LANES : (k + 1) * LANES]
            c_im = chi[rows, SIZE + k * LANES : SIZE + (k + 1) * LANES]
            x_re = window[j, 0, s : s + STRIP, cols]
            x_im = window[j, 1, s : s + STRIP, cols]
            term[0, s : s + STRIP, cols] += x_re * c_re + x_im * c_im
            term[1, s : s + STRIP, cols] += x_re * c_im - x_im * c_re
            p_re = probe[0, s : s + STRIP, cols]
            p_im = probe[1, s : s + STRIP, cols]
            g_re = (p_re * c_re + p_im * c_im).astype(BF16).astype(F32)
            g_im = (p_re * c_im - p_im * c_re).astype(BF16).astype(F32)
            turned[0].append(pltpu.roll(g_re, shift, 1))
            turned[1].append(pltpu.roll(g_im, shift, 1))
        here = slice(SIZE + s, SIZE + s + STRIP)
        for p in range(2):
            low, high = turned[p]
            spread[j, p, 0, here, :] = jnp.where(later, low, zero)
            spread[j, p, 1, here, :] = jnp.where(later, high, low)
            spread[j, p, 2, here, :] = jnp.where(later, zero, high)


def accumulate(meta_row, spread, acc):
    starts = [SIZE - jnp.bitwise_and(meta_row[j], 2 * SIZE - 1) for j in range(2)]
    for p in range(2):
        for k in range(3):
            for s in range(0, 2 * SIZE, STRIP):
                acc[p, k, s : s + STRIP, :] += (
                    spread[0, p, k, pl.ds(starts[0] + s, STRIP), :]
                    + spread[1, p, k, pl.ds(starts[1] + s, STRIP), :]
                )


MESH = pl.DeviceIdType.MESH


ORDER = (
    (0, 0),
    (0, 1), (0, 3), (1, 0), (3, 0),
    (1, 1), (3, 3), (1, 3), (3, 1),
    (1, 2), (3, 2), (2, 0),
    (2, 1), (2, 3), (0, 2),
    (2, 2),
)
AT_ONCE = 4
STARTED = (6, 6, 8, 8, 11, 11, 11, 14, 15, 15, 15, 15, 15, 15, 15, 15)


def chosen(s, table):
    return sum(jnp.where(s == i, v, 0) for i, v in enumerate(table) if v)


def fused_kernel(
    n_pos, n_obj, scale,
    owner, rows, cols, amps_hbm, obj_hbm, probe_hbm, left_hbm, right_hbm,
    object_out, probe_out,
    amps, probe, left, right,
    slots, landed, meta_out, meta_in, meta, tile, window, psi, half, wave, diff, chi, spread, acc,
    term, exact, rounded, got_a, got_b, all_a, all_b, done, picked, ext, edge_out, edge_in, sides,
    load_sem, amp_send, amp_recv, meta_send, meta_recv, meta_sem, sum_send, sum_recv,
    halo_send, halo_recv,
):
    tall = 2 * SIZE
    inner = ext.at[:, pl.ds(8, tall), :]
    loads = [
        pltpu.make_async_copy(source, target, load_sem.at[i])
        for i, (source, target) in enumerate(
            ((amps_hbm, amps), (obj_hbm, inner), (probe_hbm, probe), (left_hbm, left), (right_hbm, right))
        )
    ]
    for c in loads:
        c.start()
    me_p = lax.axis_index("pos")
    me_o = lax.axis_index("obj")
    side = math.isqrt(n_pos)
    peer_o = [lax.rem(me_o + d, n_obj) for d in range(1, n_obj)]


    def peer_at(s):
        if isinstance(s, int):
            dx, dy = ORDER[s]
        else:
            dx = chosen(s, [d[0] for d in ORDER])
            dy = chosen(s, [d[1] for d in ORDER])
        x = lax.rem(me_p // side + dx, side)
        y = lax.rem(me_p % side + dy, side)
        return x * side + y

    peer_p = [peer_at(s) for s in range(1, n_pos)]

    barrier = pltpu.get_barrier_semaphore()
    for o in peer_o:
        pl.semaphore_signal(barrier, inc=1, device_id=(me_p, o), device_id_type=MESH)
    for p in peer_p:
        pl.semaphore_signal(barrier, inc=1, device_id=(p, me_o), device_id_type=MESH)

    def amp_copy(s):
        return pltpu.make_async_remote_copy(
            src_ref=slots.at[s], dst_ref=landed.at[s],
            send_sem=amp_send.at[s], recv_sem=amp_recv.at[s],
            device_id=(peer_at(s), me_o), device_id_type=MESH,
        )

    def meta_copy(s):
        return pltpu.make_async_remote_copy(
            src_ref=meta_out.at[s], dst_ref=meta_in.at[s],
            send_sem=meta_send.at[s], recv_sem=meta_recv.at[s],
            device_id=(peer_at(s), me_o), device_id_type=MESH,
        )

    lane = lax.broadcasted_iota(jnp.int32, (8, LANES), 1)

    def announce(s, corners):
        target = peer_at(s)
        first = jnp.int32(-1)
        second = jnp.int32(-1)
        for i in reversed(range(amps.shape[0])):
            hit = owner[i] == target
            second = jnp.where(hit, first, second)
            first = jnp.where(hit, i, first)
        values = jnp.zeros((8, LANES), jnp.int32)
        for k, found in enumerate((first, second)):
            i = jnp.maximum(found, 0)
            picked[s, k] = i
            row = jnp.where(found < 0, 2 * SIZE, rows[i])
            values = jnp.where(lane == 2 * k, row, values)
            values = jnp.where(lane == 2 * k + 1, cols[i], values)
        corners[s] = values

    def lay_out(s, out):
        for k in range(CAPACITY):
            out[s, k] = amps[picked[s, k]]

    def send(s):
        lay_out(s, slots)
        amp_copy(s).start()

    @pl.loop(1, n_pos)
    def _(s):
        announce(s, meta_out)

    loads[0].wait()

    @pl.loop(1, 1 + AT_ONCE)
    def _(s):
        lay_out(s, slots)

    pl.semaphore_wait(barrier, n_obj + n_pos - 2)

    @pl.loop(1, 1 + AT_ONCE)
    def _(s):
        amp_copy(s).start()

    @pl.loop(1, n_pos)
    def _(s):
        meta_copy(s).start()

    announce(0, meta_in)
    lay_out(0, landed)
    loads[1].wait()

    next_p, last_p = lax.rem(me_p + 1, n_pos), lax.rem(me_p + n_pos - 1, n_pos)
    next_o, last_o = lax.rem(me_o + 1, n_obj), lax.rem(me_o + n_obj - 1, n_obj)

    def halo(i, source, target, device):
        return pltpu.make_async_remote_copy(
            src_ref=source, dst_ref=target, send_sem=halo_send.at[i], recv_sem=halo_recv.at[i],
            device_id=device, device_id_type=MESH,
        )

    for p in range(2):
        edge_out[0, p] = ext[p, 8 : tall + 8, 2 * LANES : 3 * LANES].T[LANES - 8 : LANES]
        edge_out[1, p] = ext[p, 8 : tall + 8, 0:LANES].T[0:8]
    halos = [
        halo(0, ext.at[:, pl.ds(tall, 8), :], ext.at[:, pl.ds(0, 8), :], (me_p, next_o)),
        halo(1, ext.at[:, pl.ds(8, 8), :], ext.at[:, pl.ds(tall + 8, 8), :], (me_p, last_o)),
        halo(2, edge_out.at[0], edge_in.at[0], (next_p, me_o)),
        halo(3, edge_out.at[1], edge_in.at[1], (last_p, me_o)),
    ]
    for c in halos:
        c.start()
    for p in range(2):
        for k in range(3):
            block = slice(k * LANES, (k + 1) * LANES)
            tile[p, k, 0 : 2 * SIZE, :] = ext[p, 8 : tall + 8, block].astype(BF16).astype(F32)
            tile[p, k, 2 * SIZE : 3 * SIZE, :] = jnp.zeros((SIZE, LANES), F32)
            for j in range(2):
                spread[j, p, k, 0:SIZE, :] = jnp.zeros((SIZE, LANES), F32)
                spread[j, p, k, 2 * SIZE : 3 * SIZE, :] = jnp.zeros((SIZE, LANES), F32)
    acc[...] = jnp.zeros_like(acc)
    term[...] = jnp.zeros_like(term)

    @pl.loop(1, n_pos)
    def _(s):
        meta_copy(s).wait()

    to_scalars = pltpu.make_async_copy(meta_in, meta, meta_sem)
    to_scalars.start()
    to_scalars.wait()
    for c in loads[2:]:
        c.wait()

    @pl.loop(0, n_pos)
    def _(s):
        @pl.loop(chosen(s, (AT_ONCE,) + STARTED[:-1]) + 1, chosen(s, STARTED) + 1)
        def _(m):
            send(m)

        @pl.when(s > 0)
        def _():
            accumulate([meta[s - 1, 0, 2 * j] for j in range(2)], spread, acc)
            amp_copy(s).wait_recv()

        row = [meta[s, 0, 2 * j] for j in range(2)]
        col = [meta[s, 0, 2 * j + 1] for j in range(2)]
        amp = landed.at[s]
        for j in range(2):
            extract(row[j], col[j], tile, probe, window, psi, j)
        turn(jnp.dot(left[...], psi[...], preferred_element_type=F32), half)
        wave[...] = jnp.dot(half[...], right[...], preferred_element_type=F32)
        for j in range(2):
            modulus(wave, amp, diff, j)
        turn(jnp.dot(right[...], diff[...], preferred_element_type=F32), half)
        chi[...] = jnp.dot(half[...], left[...], preferred_element_type=F32)
        for j in range(2):
            gradients(col[j], chi, probe, window, spread, term, j)

    across = SIZE // LANES
    for plane in range(2):
        for i in range(SIZE // 16):
            for k in range(across):
                values = term[plane, 16 * i : 16 * i + 16, k * LANES : (k + 1) * LANES]
                exact[(plane * (SIZE // 16) + i) * across + k] = values
                rounded[(plane * (SIZE // 16) + i) * across + k] = values.astype(BF16)

    first = SIZE // 16 * across
    a_size, b_size = first // n_obj, first // n_pos
    of_a = lambda o: pl.ds(o * a_size, a_size)
    of_b = lambda p: pl.ds(first + p * b_size, b_size)

    def phase(base, a_of, b_of):
        copies = []
        for d, p in reversed(list(enumerate(peer_p))) if b_of else ():
            copies.append(((p, me_o), *b_of(d, p)))
        for d, o in enumerate(peer_o) if a_of else ():
            copies.append(((me_p, o), *a_of(d, o)))
        copies = [
            pltpu.make_async_remote_copy(
                src_ref=source, dst_ref=target,
                send_sem=sum_send.at[base + i], recv_sem=sum_recv.at[base + i],
                device_id=device, device_id_type=MESH,
            )
            for i, (device, source, target) in enumerate(copies)
        ]
        for c in copies:
            c.start()
        return copies

    step = n_obj - 1 + n_pos - 1
    one = phase(
        0,
        lambda d, o: (rounded.at[of_a(o)], got_a.at[d]),
        lambda d, p: (rounded.at[of_b(p)], got_b.at[d]),
    )
    accumulate([meta[n_pos - 1, 0, 2 * j] for j in range(2)], spread, acc)
    for c in halos:
        c.wait()
    middle = jnp.zeros((LANES - 16, tall), F32)
    for p in range(2):
        sides[p] = jnp.concatenate([edge_in[1, p], middle, edge_in[0, p]], axis=0).T
    lanes = lax.broadcasted_iota(jnp.int32, (STRIP, LANES), 1)
    for p in range(2):
        for s in range(0, tall, STRIP):
            here = [ext[p, 8 + s : 8 + s + STRIP, k * LANES : (k + 1) * LANES] for k in range(3)]
            here.append(sides[p, s : s + STRIP, :])
            right_of = [pltpu.roll(t, LANES - 1, 1) for t in here]
            left_of = [pltpu.roll(t, 1, 1) for t in here]
            for k in range(3):
                block = slice(k * LANES, (k + 1) * LANES)
                around = ext[p, 7 + s : 7 + s + STRIP, block] + ext[p, 9 + s : 9 + s + STRIP, block]
                around += jnp.where(lanes == 0, left_of[k - 1], left_of[k])
                around += jnp.where(lanes == LANES - 1, right_of[k + 1], right_of[k])
                object_out[p, s : s + STRIP, block] = (
                    0.5 * here[k] + 0.125 * around - 0.25 * acc[p, k, s : s + STRIP, :]
                )


    @pl.loop(1, n_pos)
    def _(s):
        amp_copy(s).wait_send()

    for c in one[n_pos - 1 :]:
        c.wait_recv()
    total = exact[of_a(me_o)]
    for d in range(n_obj - 1):
        total += got_a[d].astype(F32)
    all_a[me_p] = total.astype(BF16)
    two = phase(step, None, lambda d, p: (all_a.at[me_p], all_a.at[me_p]))
    for c in one[: n_pos - 1]:
        c.wait_recv()
    total = exact[of_b(me_p)]
    for d in range(n_pos - 1):
        total += got_b[d].astype(F32)
    all_b[me_o] = total.astype(BF16)
    more = phase(step + n_pos - 1, lambda d, o: (all_b.at[me_o], all_b.at[me_o]), None)
    for c in more:
        c.wait_recv()
    total = all_b[0].astype(F32)
    for d in range(1, n_obj):
        total += all_b[d].astype(F32)
    done[of_b(me_p)] = total
    three = phase(2 * step, None, lambda d, p: (done.at[of_b(me_p)], done.at[of_b(me_p)]))
    for c in two:
        c.wait_recv()
    total = all_a[0].astype(F32)
    for d in range(1, n_pos):
        total += all_a[d].astype(F32)
    done[of_a(me_o)] = total
    last = phase(
        2 * step + n_pos - 1, lambda d, o: (done.at[of_a(me_o)], done.at[of_a(me_o)]), None
    )
    for c in three + last:
        c.wait_recv()
    for plane in range(2):
        for i in range(SIZE // 16):
            for k in range(across):
                here, block = slice(16 * i, 16 * i + 16), slice(k * LANES, (k + 1) * LANES)
                probe_out[plane, here, block] = probe[plane, here, block] - scale * done[
                    (plane * (SIZE // 16) + i) * across + k
                ]
    for c in one + two + more + three + last:
        c.wait_send()


def fused(owner, rows, cols, amps, obj, probe, left, right, n_pos, n_obj, scale):
    smem = pl.BlockSpec(memory_space=pltpu.SMEM)
    vmem = pl.BlockSpec(memory_space=pltpu.VMEM)
    hbm = pl.BlockSpec(memory_space=pl.ANY)
    count = 3 * (n_pos + n_obj - 2)
    pieces = 2 * SIZE * SIZE // (16 * LANES)
    a_size, b_size = pieces // 2 // n_obj, pieces // 2 // n_pos
    double = (2 * SIZE, 2 * SIZE)
    dma = pltpu.SemaphoreType.DMA
    return pl.pallas_call(
        functools.partial(fused_kernel, n_pos, n_obj, scale),
        out_shape=(
            pltpu.VMEM(obj.shape, F32),
            pltpu.VMEM(probe.shape, F32),
        ),
        in_specs=[smem, smem, smem, hbm, hbm, hbm, hbm, hbm],
        out_specs=(vmem, vmem),
        scratch_shapes=[
            pltpu.VMEM(amps.shape, BF16),
            pltpu.VMEM(probe.shape, F32),
            pltpu.VMEM(double, BF16),
            pltpu.VMEM(double, BF16),
            pltpu.VMEM((n_pos, CAPACITY, SIZE, SIZE), BF16),
            pltpu.VMEM((n_pos, CAPACITY, SIZE, SIZE), BF16),
            pltpu.VMEM((n_pos, 8, LANES), jnp.int32),
            pltpu.VMEM((n_pos, 8, LANES), jnp.int32),
            pltpu.SMEM((n_pos, 8, LANES), jnp.int32),
            pltpu.VMEM((2, 3, 3 * SIZE, LANES), F32),
            pltpu.VMEM((2, 2, SIZE, SIZE), F32),
            pltpu.VMEM(double, BF16),
            pltpu.VMEM(double, BF16),
            pltpu.VMEM(double, F32),
            pltpu.VMEM(double, BF16),
            pltpu.VMEM(double, F32),
            pltpu.VMEM((2, 2, 3, 3 * SIZE, LANES), F32),
            pltpu.VMEM((2, 3, 2 * SIZE, LANES), F32),
            pltpu.VMEM((2, SIZE, SIZE), F32),
            pltpu.VMEM((pieces, 16, LANES), F32),
            pltpu.VMEM((pieces, 16, LANES), BF16),
            pltpu.VMEM((n_obj - 1, a_size, 16, LANES), BF16),
            pltpu.VMEM((n_pos - 1, b_size, 16, LANES), BF16),
            pltpu.VMEM((n_pos, a_size, 16, LANES), BF16),
            pltpu.VMEM((n_obj, b_size, 16, LANES), BF16),
            pltpu.VMEM((pieces, 16, LANES), F32),
            pltpu.SMEM((n_pos, CAPACITY), jnp.int32),
            pltpu.VMEM((2, 2 * SIZE + 16, 3 * LANES), F32),
            pltpu.VMEM((2, 2, 8, 2 * SIZE), F32),
            pltpu.VMEM((2, 2, 8, 2 * SIZE), F32),
            pltpu.VMEM((2, 2 * SIZE, LANES), F32),
            dma((5,)), dma((n_pos,)), dma((n_pos,)), dma((n_pos,)), dma((n_pos,)), dma,
            dma((count,)), dma((count,)), dma((4,)), dma((4,)),
        ],
        compiler_params=pltpu.CompilerParams(
            collective_id=1, has_side_effects=True, vmem_limit_bytes=52 << 20
        ),
        cost_estimate=pl.CostEstimate(
            flops=2 * n_pos * 32 * SIZE**3, bytes_accessed=16 << 20, transcendentals=0
        ),
        name="fused",
    )(owner, rows, cols, amps, obj, probe, left, right)


def shards(object_field, probe, amplitude, row_offset, col_offset, owner):
    n_pos = lax.axis_size("pos")
    n_obj = lax.axis_size("obj")
    pos_dev = amplitude.shape[0]
    left, right = dft_blocks()
    scale = 1.0 / math.sqrt(pos_dev * n_pos * n_obj)
    return fused(
        owner, row_offset, col_offset, amplitude, object_field, probe, left, right,
        n_pos, n_obj, scale,
    )


def solution(mesh):
    placed = (
        P(None, "obj", "pos"),
        P(),
        P(("pos", "obj"), None, None),
        P(("pos", "obj")),
        P(("pos", "obj")),
        P(("pos", "obj")),
    )
    return jax.shard_map(
        shards, mesh=mesh, in_specs=placed, out_specs=(P(None, "obj", "pos"), P()), check_vma=False
    )
```
